256 devices in a mesh: chrom: 4 (over x), snp: 64 (over z, y, core).
Axes of the slice: x: 4, y: 4, z: 8, core: 2. Of those that a mesh axis runs over, the one named last changes fastest.
Arguments:
- genotypes: bfloat16 [12288, 131072], P(None, ('chrom', 'snp')), may hold values from 0 to 2, as said below
- probes: bfloat16 [131072, 128], P(('chrom', 'snp')), may hold values from -4 to 4
Outputs:
- unit_basis: float32 [131072, 128], P(('chrom', 'snp'))
- range_log_norms: float32 [128], replicated
The draws below stay inside these ranges and needn't reach their ends.
Inputs may be any that keep to these rules, and one draw needn't show every extreme that they name: `genotypes`: every entry is a dosage 0, 1 or 2.
All inputs are finite; a program needn't handle non-finite values.
Results may differ from the reference program's by a relative error of at most 0.0034.
The reference program's roundings to bfloat16 on the way (of `scaled`, `sketch_high`, `sketch_mid` and `sketch_low`) count: a program that leaves them out, or rounds other values in their place, can miss the bound.
Values sent between devices are 32-bit elements; how exact they have to be, the bound alone decides.
No kernel may reach another device: no remote copies, remote signals or barrier semaphores. Data moves between devices by JAX's collectives and lax.ppermute only.
A program may use at most 128 MiB of HBM per device.

```python
import math
import jax
import jax.numpy as jnp
from jax import lax

SAMPLES = 12288
SNP_DEV = 512
PROBES = 128
SNPS = 131072


def draw_genotypes(key, part):
    freq_key = jax.random.fold_in(key, 11)
    first_key = jax.random.fold_in(key, 12)
    second_key = jax.random.fold_in(key, 13)
    position = jnp.arange(SNPS, dtype=jnp.float32) / SNPS
    jitter = jax.random.uniform(freq_key, (SNPS,), jnp.float32, 0.5, 1.0)
    frequency = jnp.exp(jnp.log(0.02) + position * jnp.log(25.0)) * jitter
    frequency = jnp.broadcast_to(frequency[None, :], (SAMPLES, SNPS))
    first_allele = (jax.random.uniform(first_key, (SAMPLES, SNPS), jnp.float32) < frequency).astype(jnp.float32)
    second_allele = (jax.random.uniform(second_key, (SAMPLES, SNPS), jnp.float32) < frequency).astype(jnp.float32)
    return (first_allele + second_allele).astype(jnp.bfloat16)


def draw_probes(key, part):
    shared_key = jax.random.fold_in(key, 21)
    noise_key = jax.random.fold_in(key, 22)
    shared = jnp.clip(jax.random.normal(shared_key, (SNPS, 1), jnp.float32), -4.0, 4.0)
    noise = jax.random.normal(noise_key, (SNPS, PROBES), jnp.float32)
    values = jnp.clip(shared + noise / 56.0, -4.0, 4.0)
    return values.astype(jnp.bfloat16)


def setup_inputs(seed: int = 0) -> dict:
    streams_of = jax.random.split(jax.random.key(seed), 3)
    genotypes = draw_genotypes(jax.random.fold_in(streams_of[2], 71), 0)
    probes = draw_probes(jax.random.fold_in(streams_of[2], 71), 0)
    return {"genotypes": genotypes, "probes": probes}


def standardize(block):
    values = block.astype(jnp.float32)
    column_mean = lax.optimization_barrier(jnp.mean(values, axis=0, keepdims=True))
    centered = values - column_mean
    spread = lax.optimization_barrier(jnp.mean(centered * centered, axis=0, keepdims=True))
    return (centered * (spread + 1e-05) ** (-0.125)).astype(jnp.bfloat16)

def split_parts(sketch):
    sketch_high = lax.optimization_barrier(sketch.astype(jnp.bfloat16))
    remainder = sketch - sketch_high.astype(jnp.float32)
    sketch_mid = lax.optimization_barrier(remainder.astype(jnp.bfloat16))
    sketch_low = (remainder - sketch_mid.astype(jnp.float32)).astype(jnp.bfloat16)
    return jnp.concatenate([sketch_high, sketch_mid, sketch_low], axis=1)

def column_gram(matrix):
    return lax.dot_general(matrix.astype(jnp.float32), matrix.astype(jnp.float32), (((0,), (0,)), ((), ())), precision=lax.Precision.HIGHEST, preferred_element_type=jnp.float32)

def unit_columns(matrix, gram_matrix):
    lower_factor = jnp.linalg.cholesky(gram_matrix)
    return lax.linalg.triangular_solve(lower_factor, matrix, left_side=False, lower=True, transpose_a=True)

def reference(genotypes, probes):
    blocks = SNPS // SNP_DEV
    block_ids = jnp.arange(blocks, dtype=jnp.int32)

    def add_block(running, block_index):
        offset = (block_index * SNP_DEV).astype(jnp.int32)
        columns = lax.dynamic_slice_in_dim(genotypes, offset, SNP_DEV, 1)
        probe_rows = lax.dynamic_slice_in_dim(probes, offset, SNP_DEV, 0)
        scaled = standardize(columns)
        return (running + jnp.dot(scaled.astype(jnp.float32), probe_rows.astype(jnp.float32), preferred_element_type=jnp.float32), None)
    sketch, _ = lax.scan(add_block, jnp.zeros((SAMPLES, PROBES), jnp.float32), block_ids)
    sketch_parts = split_parts(sketch)

    def project(block_index):
        offset = (block_index * SNP_DEV).astype(jnp.int32)
        columns = lax.dynamic_slice_in_dim(genotypes, offset, SNP_DEV, 1)
        scaled = standardize(columns)
        product = lax.dot_general(scaled.astype(jnp.float32), sketch_parts.astype(jnp.float32), (((0,), (0,)), ((), ())), preferred_element_type=jnp.float32)
        return product[:, :PROBES] + product[:, PROBES:2 * PROBES] + product[:, 2 * PROBES:]
    range_rows = lax.map(project, block_ids).reshape(SNPS, PROBES)
    gram_first = column_gram(range_rows)
    range_log_norms = 0.1 * jnp.log(jnp.diagonal(gram_first) / SNPS)
    first_basis = unit_columns(range_rows, gram_first)
    second_basis = unit_columns(first_basis, column_gram(first_basis))
    return (second_basis * math.sqrt(SNPS), range_log_norms)
```

```python
import math

import jax
import jax.numpy as jnp
from jax import lax
from jax.sharding import Mesh
from jax.sharding import PartitionSpec as P

AXES = ("x", "z", "y", "c")


def pair_list(sizes, move):
    nx, nz, ny, nc = sizes
    pairs = []
    for x in range(nx):
        for z in range(nz):
            for y in range(ny):
                for c in range(nc):
                    X, Z, Y, C = move(x, z, y, c)
                    src = ((x * nz + z) * ny + y) * nc + c
                    dst = (((X % nx) * nz + Z % nz) * ny + Y % ny) * nc + C % nc
                    pairs.append((src, dst))
    return pairs


class Torus:
    def __init__(self, sizes):
        self.sizes = sizes

    def core(self, value):
        return lax.ppermute(value, AXES, pair_list(self.sizes, lambda x, z, y, c: (x, z, y, c + 1)))

    def first(self, value, k):
        def move(x, z, y, c):
            return (x + k, z, y, c) if c == 0 else (x, z, y + k, c)

        return lax.ppermute(value, AXES, pair_list(self.sizes, move))

    def second(self, value, k):
        def move(x, z, y, c):
            return (x, z, y + k, c) if c == 0 else (x + k, z, y, c)

        return lax.ppermute(value, AXES, pair_list(self.sizes, move))

    def places(self):
        core, x, y = lax.axis_index("c"), lax.axis_index("x"), lax.axis_index("y")
        return core, jnp.where(core == 0, x, y), jnp.where(core == 0, y, x)


def take(blocks, index):
    return lax.dynamic_index_in_dim(blocks, index, 0, keepdims=False)


def scatter_ring(blocks, place, send):
    got = [send(take(blocks, (place + k) % 4), k) for k in (1, 2, 3)]
    return (take(blocks, place) + got[1]) + (got[0] + got[2])


def gather_ring(block, place, send):
    got = [send(block, k) for k in (1, 2, 3)]
    out = jnp.zeros((4, *block.shape), block.dtype)
    for k, piece in enumerate([block, *got]):
        out = lax.dynamic_update_index_in_dim(out, piece, (place - k) % 4, 0)
    return out


def sum_tall(torus, partial):
    rows, width = partial.shape
    core, one, two = torus.places()
    halves = partial.reshape(2, rows // 2, width)
    half = take(halves, core) + torus.core(take(halves, 1 - core))
    quarter = scatter_ring(half.reshape(4, rows // 8, width), one, torus.first)
    small = scatter_ring(quarter.reshape(4, rows // 32, width), two, torus.second)
    depth = torus.sizes[1]
    own = lax.all_to_all(small.reshape(depth, rows // 32 // depth, width), "z", 0, 0).sum(0)
    small = lax.all_to_all(jnp.broadcast_to(own, (depth, *own.shape)), "z", 0, 0)
    quarter = gather_ring(small.reshape(rows // 32, width), two, torus.second)
    half = gather_ring(quarter.reshape(rows // 8, width), one, torus.first).reshape(rows // 2, width)
    other = torus.core(half)
    return jnp.where(core == 0, jnp.stack([half, other]), jnp.stack([other, half])).reshape(rows, width)


def sum_ring(value, send):
    got = [send(value, k) for k in (1, 2, 3)]
    return (value + got[1]) + (got[0] + got[2])


def sum_square(torus, partial):
    rows, width = partial.shape
    core = lax.axis_index("c")
    halves = partial.reshape(2, rows // 2, width)
    half = take(halves, core) + torus.core(take(halves, 1 - core))
    half = sum_ring(half, torus.first)
    half = sum_ring(half, torus.second)
    depth = torus.sizes[1]
    half = lax.all_to_all(jnp.broadcast_to(half, (depth, *half.shape)), "z", 0, 0).sum(0)
    other = torus.core(half)
    return jnp.where(core == 0, jnp.stack([half, other]), jnp.stack([other, half])).reshape(rows, width)


def standardize(block):
    values = block.astype(jnp.float32)
    column_mean = jnp.mean(values, axis=0, keepdims=True)
    centered = values - column_mean
    spread = jnp.mean(centered * centered, axis=0, keepdims=True)
    return (centered * (spread + 1e-05) ** (-0.125)).astype(jnp.bfloat16)


def split_parts(sketch):
    sketch_high = lax.optimization_barrier(sketch.astype(jnp.bfloat16))
    remainder = sketch - sketch_high.astype(jnp.float32)
    sketch_mid = lax.optimization_barrier(remainder.astype(jnp.bfloat16))
    sketch_low = (remainder - sketch_mid.astype(jnp.float32)).astype(jnp.bfloat16)
    return jnp.concatenate([sketch_high, sketch_mid, sketch_low], axis=1)


def column_gram(matrix):
    return lax.dot_general(
        matrix,
        matrix,
        (((0,), (0,)), ((), ())),
        precision=lax.Precision.HIGHEST,
        preferred_element_type=jnp.float32,
    )


def unit_columns(matrix, gram_matrix):
    lower_factor = jnp.linalg.cholesky(gram_matrix)
    return lax.linalg.triangular_solve(
        lower_factor, matrix, left_side=False, lower=True, transpose_a=True
    )


def solution(mesh):
    nx = mesh.shape["chrom"]
    nz = mesh.shape["snp"] // 8
    torus = Torus((nx, nz, 4, 2))
    fine = Mesh(mesh.devices.reshape(torus.sizes), AXES)

    def body(genotypes, probes):
        scaled = standardize(genotypes)
        width = probes.shape[1]
        sketch = sum_tall(torus, jnp.dot(scaled, probes, preferred_element_type=jnp.float32))
        sketch_parts = split_parts(sketch)
        product = lax.dot_general(
            scaled, sketch_parts, (((0,), (0,)), ((), ())), preferred_element_type=jnp.float32
        )
        range_rows = product[:, :width] + product[:, width : 2 * width] + product[:, 2 * width :]
        total_snps = range_rows.shape[0] * fine.size
        gram_first = sum_square(torus, column_gram(range_rows))
        diagonal = jnp.sum(gram_first * jnp.eye(width, dtype=jnp.float32), axis=0)
        range_log_norms = 0.1 * jnp.log(diagonal / total_snps)
        first_basis = unit_columns(range_rows, gram_first)
        gram_second = sum_square(torus, column_gram(first_basis))
        second_basis = unit_columns(first_basis, gram_second)
        return (second_basis * math.sqrt(total_snps), range_log_norms)

    return jax.shard_map(
        body,
        mesh=fine,
        in_specs=(P(None, AXES), P(AXES, None)),
        out_specs=(P(AXES, None), P()),
        check_vma=False,
    )
```

```python
import functools
import math

import jax
import jax.numpy as jnp
from jax import lax
from jax.experimental import pallas as pl
from jax.experimental.pallas import tpu as pltpu
from jax.sharding import Mesh
from jax.sharding import PartitionSpec as P

AXES = ("x", "z", "y", "c")


def pair_list(sizes, move):
    nx, nz, ny, nc = sizes
    pairs = []
    for x in range(nx):
        for z in range(nz):
            for y in range(ny):
                for c in range(nc):
                    X, Z, Y, C = move(x, z, y, c)
                    src = ((x * nz + z) * ny + y) * nc + c
                    dst = (((X % nx) * nz + Z % nz) * ny + Y % ny) * nc + C % nc
                    pairs.append((src, dst))
    return pairs


class Torus:
    def __init__(self, sizes):
        self.sizes = sizes

    def core(self, value):
        return lax.ppermute(value, AXES, pair_list(self.sizes, lambda x, z, y, c: (x, z, y, c + 1)))

    def first(self, value, k):
        def move(x, z, y, c):
            return (x + k, z, y, c) if c == 0 else (x, z, y + k, c)

        return lax.ppermute(value, AXES, pair_list(self.sizes, move))

    def second(self, value, k):
        def move(x, z, y, c):
            return (x, z, y + k, c) if c == 0 else (x + k, z, y, c)

        return lax.ppermute(value, AXES, pair_list(self.sizes, move))

    def places(self):
        core, x, y = lax.axis_index("c"), lax.axis_index("x"), lax.axis_index("y")
        return core, jnp.where(core == 0, x, y), jnp.where(core == 0, y, x)


def take(blocks, index):
    return lax.dynamic_index_in_dim(blocks, index, 0, keepdims=False)


def scatter_ring(blocks, place, send):
    got = [send(take(blocks, (place + k) % 4), k) for k in (1, 2, 3)]
    return (take(blocks, place) + got[1]) + (got[0] + got[2])


def gather_ring(block, place, send):
    got = [send(block, k) for k in (1, 2, 3)]
    out = jnp.zeros((4, *block.shape), block.dtype)
    for k, piece in enumerate([block, *got]):
        out = lax.dynamic_update_index_in_dim(out, piece, (place - k) % 4, 0)
    return out


def sum_tall(torus, partial):
    rows, width = partial.shape
    core, one, two = torus.places()
    halves = partial.reshape(2, rows // 2, width)
    half = take(halves, core) + torus.core(take(halves, 1 - core))
    quarter = scatter_ring(half.reshape(4, rows // 8, width), one, torus.first)
    small = scatter_ring(quarter.reshape(4, rows // 32, width), two, torus.second)
    depth = torus.sizes[1]
    own = lax.all_to_all(small.reshape(depth, rows // 32 // depth, width), "z", 0, 0).sum(0)
    small = lax.all_to_all(jnp.broadcast_to(own, (depth, *own.shape)), "z", 0, 0)
    quarter = gather_ring(small.reshape(rows // 32, width), two, torus.second)
    half = gather_ring(quarter.reshape(rows // 8, width), one, torus.first).reshape(rows // 2, width)
    other = torus.core(half)
    return jnp.where(core == 0, jnp.stack([half, other]), jnp.stack([other, half])).reshape(rows, width)


def add_pairs(a, b):
    total = a[0] + b[0]
    back = total - a[0]
    lost = (a[0] - (total - back)) + (b[0] - back)
    return jnp.stack([total, (a[1] + b[1]) + lost])


def sum_ring(value, send):
    got = [send(value, k) for k in (1, 2, 3)]
    return add_pairs(add_pairs(value, got[1]), add_pairs(got[0], got[2]))


def sum_square(torus, pair):
    _, rows, width = pair.shape
    core = lax.axis_index("c")
    halves = pair.reshape(2, 2, rows // 2, width).swapaxes(0, 1)
    half = add_pairs(take(halves, core), torus.core(take(halves, 1 - core)))
    half = sum_ring(half, torus.first)
    half = sum_ring(half, torus.second)
    depth = torus.sizes[1]
    got = lax.all_to_all(jnp.broadcast_to(half, (depth, *half.shape)), "z", 0, 0)
    terms = [got[i] for i in range(depth)]
    while len(terms) > 1:
        terms = [add_pairs(*terms[i : i + 2]) for i in range(0, len(terms), 2)]
    half = terms[0]
    other = torus.core(half)
    both = jnp.where(core == 0, jnp.stack([half, other]), jnp.stack([other, half]))
    return both.swapaxes(0, 1).reshape(2, rows, width)


SLICES = 5


def cut(values, peak):
    sigma = peak * 131072.0
    slices = []
    for _ in range(SLICES):
        part = (values + sigma) - sigma
        slices.append(part.astype(jnp.bfloat16))
        values = values - part
        sigma = sigma * 0.0078125
    return slices


def exact_gram(values):
    flipped = values.T
    right = cut(values, jnp.max(jnp.abs(values), axis=0, keepdims=True))
    left = cut(flipped, jnp.max(jnp.abs(flipped), axis=1, keepdims=True))
    hi = jnp.zeros((values.shape[1], values.shape[1]), jnp.float32)
    lo = jnp.zeros_like(hi)
    for level in reversed(range(SLICES + 1)):
        for i in range(SLICES):
            if 0 <= level - i < SLICES:
                term = jnp.dot(left[i], right[level - i], preferred_element_type=jnp.float32)
                total = hi + term
                back = total - hi
                lo = lo + ((hi - (total - back)) + (term - back))
                hi = total
    return hi, lo


def gram_kernel(rows_ref, out_ref):
    hi, lo = exact_gram(rows_ref[...])
    out_ref[0] = hi
    out_ref[1] = lo


def exact_dot(a, b):
    return lax.dot_general(
        a,
        b,
        (((1,), (0,)), ((), ())),
        precision=lax.Precision.HIGHEST,
        preferred_element_type=jnp.float32,
    )


def eliminate(matrix, a_ref, b_ref):
    n = matrix.shape[0]
    row = lax.broadcasted_iota(jnp.int32, (n, n), 0)
    col = lax.broadcasted_iota(jnp.int32, (n, n), 1)
    a_ref[...] = matrix
    b_ref[...] = (row == col).astype(jnp.float32)
    column_row = lax.broadcasted_iota(jnp.int32, (n, 1), 0)
    panel_row = lax.broadcasted_iota(jnp.int32, (8, 1), 0)

    def block(index, carry):
        start = pl.multiple_of(index * 8, 8)
        a, b = a_ref[...], b_ref[...]
        pa, pb = a_ref[pl.ds(start, 8), :], b_ref[pl.ds(start, 8), :]
        for t in range(8):
            inverse = 1.0 / pa[t : t + 1, t : t + 1]
            ra, rb = pa[t : t + 1, :] * inverse, pb[t : t + 1, :] * inverse
            factor = jnp.where(column_row > start + t, a[:, t : t + 1], 0.0)
            a, b = a - factor * ra, b - factor * rb
            if t < 7:
                factor = jnp.where(panel_row > t, pa[:, t : t + 1], 0.0)
                pa, pb = pa - factor * ra, pb - factor * rb
        a_ref[...] = pltpu.roll(a, n - 8, 1)
        b_ref[...] = b
        return carry

    lax.fori_loop(0, n // 8, block, 0)
    upper = jnp.where(col >= row, a_ref[...], 0.0)
    pivot = jnp.sum(jnp.where(col == row, upper, 0.0), axis=1, keepdims=True)
    root = lax.rsqrt(pivot)
    return upper * root, b_ref[...] * root


def factor_kernel(scale, count, pair_ref, basis_ref, norms_ref, a_ref, b_ref, out_ref):
    hi, lo = pair_ref[0], pair_ref[1]
    n = hi.shape[0]
    row = lax.broadcasted_iota(jnp.int32, (n, n), 0)
    col = lax.broadcasted_iota(jnp.int32, (n, n), 1)
    eye = row == col
    total = hi + lo
    lo = (hi - total) + lo
    hi = total
    diagonal = jnp.sum(jnp.where(eye, hi, 0.0), axis=0, keepdims=True)
    norms_ref[...] = 0.1 * jnp.log(diagonal / count)
    upper, below = eliminate(hi, a_ref, b_ref)
    back_hi, back_lo = exact_gram(upper)
    rest = ((hi - back_hi) - back_lo) + lo
    above = below.T
    rest = exact_dot(exact_dot(below, rest), above)
    size = jnp.sum(rest * rest)

    @pl.when(size < 0.01)
    def _():
        half = jnp.where(eye, 0.5, jnp.where(col > row, 1.0, 0.0))
        step = half * rest
        for _ in range(5):
            step = half * (rest - exact_dot(step.T, step))
        unit = eye.astype(jnp.float32)
        inverse = unit - step
        whole = unit + step
        for _ in range(2):
            inverse = exact_dot(inverse, 2.0 * unit - exact_dot(whole, inverse))
        out_ref[...] = inverse

    @pl.when(jnp.logical_not(size < 0.01))
    def _():
        _, small = eliminate(eye.astype(jnp.float32) + rest, a_ref, b_ref)
        out_ref[...] = small.T

    basis_ref[...] = scale * exact_dot(above, out_ref[...])


def local_gram(range_rows):
    width = range_rows.shape[1]
    return pl.pallas_call(
        gram_kernel,
        out_shape=jax.ShapeDtypeStruct((2, width, width), jnp.float32),
        name="local_gram",
    )(range_rows)


def two_factors(pair, total_snps):
    width = pair.shape[1]
    return pl.pallas_call(
        functools.partial(factor_kernel, math.sqrt(total_snps), float(total_snps)),
        out_shape=(
            jax.ShapeDtypeStruct((width, width), jnp.float32),
            jax.ShapeDtypeStruct((1, width), jnp.float32),
        ),
        scratch_shapes=[pltpu.VMEM((width, width), jnp.float32)] * 3,
        name="two_factors",
    )(pair)


def standardize(block):
    values = block.astype(jnp.float32)
    column_mean = jnp.mean(values, axis=0, keepdims=True)
    centered = values - column_mean
    spread = jnp.mean(centered * centered, axis=0, keepdims=True)
    return (centered * (spread + 1e-05) ** (-0.125)).astype(jnp.bfloat16)


def split_parts(sketch):
    sketch_high = lax.optimization_barrier(sketch.astype(jnp.bfloat16))
    remainder = sketch - sketch_high.astype(jnp.float32)
    sketch_mid = lax.optimization_barrier(remainder.astype(jnp.bfloat16))
    sketch_low = (remainder - sketch_mid.astype(jnp.float32)).astype(jnp.bfloat16)
    return jnp.concatenate([sketch_high, sketch_mid, sketch_low], axis=1)


def solution(mesh):
    nx = mesh.shape["chrom"]
    nz = mesh.shape["snp"] // 8
    torus = Torus((nx, nz, 4, 2))
    fine = Mesh(mesh.devices.reshape(torus.sizes), AXES)

    def body(genotypes, probes):
        scaled = standardize(genotypes)
        width = probes.shape[1]
        sketch = sum_tall(torus, jnp.dot(scaled, probes, preferred_element_type=jnp.float32))
        sketch_parts = split_parts(sketch)
        product = lax.dot_general(
            scaled, sketch_parts, (((0,), (0,)), ((), ())), preferred_element_type=jnp.float32
        )
        range_rows = product[:, :width] + product[:, width : 2 * width] + product[:, 2 * width :]
        total_snps = range_rows.shape[0] * fine.size
        pair = sum_square(torus, local_gram(range_rows))
        basis, range_log_norms = two_factors(pair, total_snps)
        return (exact_dot(range_rows, basis), range_log_norms[0])

    return jax.shard_map(
        body,
        mesh=fine,
        in_specs=(P(None, AXES), P(AXES, None)),
        out_specs=(P(AXES, None), P()),
        check_vma=False,
    )
```

```python
import functools
import math

import jax
import jax.numpy as jnp
from jax import lax
from jax.experimental import pallas as pl
from jax.experimental.pallas import tpu as pltpu
from jax.sharding import Mesh
from jax.sharding import PartitionSpec as P


AXES = ("x", "z", "y", "c")


def pair_list(sizes, move):
    nx, nz, ny, nc = sizes
    pairs = []
    for x in range(nx):
        for z in range(nz):
            for y in range(ny):
                for c in range(nc):
                    X, Z, Y, C = move(x, z, y, c)
                    src = ((x * nz + z) * ny + y) * nc + c
                    dst = (((X % nx) * nz + Z % nz) * ny + Y % ny) * nc + C % nc
                    pairs.append((src, dst))
    return pairs


class Torus:
    def __init__(self, sizes):
        self.sizes = sizes

    def core(self, value):
        return lax.ppermute(value, AXES, pair_list(self.sizes, lambda x, z, y, c: (x, z, y, c + 1)))

    def first(self, value, k):
        def move(x, z, y, c):
            return (x + k, z, y, c) if c == 0 else (x, z, y + k, c)

        return lax.ppermute(value, AXES, pair_list(self.sizes, move))

    def second(self, value, k):
        def move(x, z, y, c):
            return (x, z, y + k, c) if c == 0 else (x + k, z, y, c)

        return lax.ppermute(value, AXES, pair_list(self.sizes, move))

    def places(self):
        core, x, y = lax.axis_index("c"), lax.axis_index("x"), lax.axis_index("y")
        return core, jnp.where(core == 0, x, y), jnp.where(core == 0, y, x)


def take(blocks, index):
    return lax.dynamic_index_in_dim(blocks, index, 0, keepdims=False)


def scatter_ring(blocks, place, send):
    got = [send(take(blocks, (place + k) % 4), k) for k in (1, 2, 3)]
    return (take(blocks, place) + got[1]) + (got[0] + got[2])


def gather_ring(block, place, send):
    got = [send(block, k) for k in (1, 2, 3)]
    out = jnp.zeros((4, *block.shape), block.dtype)
    for k, piece in enumerate([block, *got]):
        out = lax.dynamic_update_index_in_dim(out, piece, (place - k) % 4, 0)
    return out


def add_pairs(a, b):
    total = a[0] + b[0]
    back = total - a[0]
    lost = (a[0] - (total - back)) + (b[0] - back)
    return jnp.stack([total, (a[1] + b[1]) + lost])


def sum_ring(value, send):
    got = [send(value, k) for k in (1, 2, 3)]
    return add_pairs(add_pairs(value, got[1]), add_pairs(got[0], got[2]))


def sum_square(torus, pair):
    _, rows, width = pair.shape
    core = lax.axis_index("c")
    halves = pair.reshape(2, 2, rows // 2, width).swapaxes(0, 1)
    half = add_pairs(take(halves, core), torus.core(take(halves, 1 - core)))
    half = sum_ring(half, torus.first)
    half = sum_ring(half, torus.second)
    depth = torus.sizes[1]
    got = lax.all_to_all(jnp.broadcast_to(half, (depth, *half.shape)), "z", 0, 0)
    terms = [got[i] for i in range(depth)]
    while len(terms) > 1:
        terms = [add_pairs(*terms[i : i + 2]) for i in range(0, len(terms), 2)]
    half = terms[0]
    other = torus.core(half)
    both = jnp.where(core == 0, jnp.stack([half, other]), jnp.stack([other, half]))
    return both.swapaxes(0, 1).reshape(2, rows, width)


SLICES = 5


def cut(values, peak):
    sigma = peak * 131072.0
    slices = []
    for _ in range(SLICES):
        part = (values + sigma) - sigma
        slices.append(part.astype(jnp.bfloat16))
        values = values - part
        sigma = sigma * 0.0078125
    return slices


def exact_gram(values):
    flipped = values.T
    right = cut(values, jnp.max(jnp.abs(values), axis=0, keepdims=True))
    left = cut(flipped, jnp.max(jnp.abs(flipped), axis=1, keepdims=True))
    hi = jnp.zeros((values.shape[1], values.shape[1]), jnp.float32)
    lo = jnp.zeros_like(hi)
    for level in reversed(range(SLICES + 1)):
        for i in range(SLICES):
            if 0 <= level - i < SLICES:
                term = jnp.dot(left[i], right[level - i], preferred_element_type=jnp.float32)
                total = hi + term
                back = total - hi
                lo = lo + ((hi - (total - back)) + (term - back))
                hi = total
    return hi, lo


def pack(square):
    n = square.shape[0]
    row = lax.broadcasted_iota(jnp.int32, (n // 2, n), 0)
    col = lax.broadcasted_iota(jnp.int32, (n // 2, n), 1)
    last = pltpu.roll(square[n // 2 :], n // 2, 1)
    diagonal = jnp.sum(jnp.where(col == row, last, 0.0), axis=0, keepdims=True)
    tail = jnp.where(lax.broadcasted_iota(jnp.int32, (16, n), 0) == 0, diagonal, 0.0)
    return jnp.concatenate([jnp.where(col >= row, square[: n // 2], last), tail], axis=0)


def unpack(packed):
    n = packed.shape[1]
    row = lax.broadcasted_iota(jnp.int32, (n, n), 0)
    col = lax.broadcasted_iota(jnp.int32, (n, n), 1)
    diagonal = pltpu.roll(packed[n // 2 : n // 2 + 8], n // 2, 1)[0:1]
    whole = jnp.concatenate([packed[: n // 2], jnp.zeros((n // 2, n), jnp.float32)], axis=0)
    flipped = whole.T
    low = pltpu.roll(pltpu.roll(whole, n // 2, 0), n // 2, 1)
    low_flipped = pltpu.roll(pltpu.roll(flipped, n // 2, 0), n // 2, 1)
    last = jnp.where(col < row, low, jnp.where(col == row, diagonal, low_flipped))
    below = jnp.where(col < n // 2, flipped, last)
    return jnp.where(row < n // 2, jnp.where(col >= row, whole, flipped), below)


def gram_kernel(range_ref, out_ref):
    hi, lo = exact_gram(range_ref[...].T)
    out_ref[0] = pack(hi)
    out_ref[1] = pack(lo)


def exact_dot(a, b):
    return lax.dot_general(
        a,
        b,
        (((1,), (0,)), ((), ())),
        precision=lax.Precision.HIGHEST,
        preferred_element_type=jnp.float32,
    )


def eliminate(matrix, a_ref, b_ref):
    n = matrix.shape[0]
    row = lax.broadcasted_iota(jnp.int32, (n, n), 0)
    col = lax.broadcasted_iota(jnp.int32, (n, n), 1)
    a_ref[...] = matrix
    b_ref[...] = (row == col).astype(jnp.float32)
    column_row = lax.broadcasted_iota(jnp.int32, (n, 1), 0)
    panel_row = lax.broadcasted_iota(jnp.int32, (8, 1), 0)

    def block(index, carry):
        start = pl.multiple_of(index * 8, 8)
        a, b = a_ref[...], b_ref[...]
        pa, pb = a_ref[pl.ds(start, 8), :], b_ref[pl.ds(start, 8), :]
        for t in range(8):
            inverse = 1.0 / pa[t : t + 1, t : t + 1]
            ra, rb = pa[t : t + 1, :] * inverse, pb[t : t + 1, :] * inverse
            factor = jnp.where(column_row > start + t, a[:, t : t + 1], 0.0)
            a, b = a - factor * ra, b - factor * rb
            if t < 7:
                factor = jnp.where(panel_row > t, pa[:, t : t + 1], 0.0)
                pa, pb = pa - factor * ra, pb - factor * rb
        a_ref[...] = pltpu.roll(a, n - 8, 1)
        b_ref[...] = b
        return carry

    lax.fori_loop(0, n // 8, block, 0)
    upper = jnp.where(col >= row, a_ref[...], 0.0)
    pivot = jnp.sum(jnp.where(col == row, upper, 0.0), axis=1, keepdims=True)
    root = lax.rsqrt(pivot)
    return upper * root, b_ref[...] * root


def factor_kernel(scale, count, pair_ref, basis_ref, norms_ref, a_ref, b_ref, out_ref):
    hi, lo = unpack(pair_ref[0]), unpack(pair_ref[1])
    n = hi.shape[0]
    row = lax.broadcasted_iota(jnp.int32, (n, n), 0)
    col = lax.broadcasted_iota(jnp.int32, (n, n), 1)
    eye = row == col
    total = hi + lo
    lo = (hi - total) + lo
    hi = total
    diagonal = jnp.sum(jnp.where(eye, hi, 0.0), axis=0, keepdims=True)
    norms_ref[...] = 0.1 * jnp.log(diagonal / count)
    upper, below = eliminate(hi, a_ref, b_ref)
    back_hi, back_lo = exact_gram(upper)
    rest = ((hi - back_hi) - back_lo) + lo
    above = below.T
    rest = exact_dot(exact_dot(below, rest), above)
    size = jnp.sum(rest * rest)

    @pl.when(size < 0.01)
    def _():
        half = jnp.where(eye, 0.5, jnp.where(col > row, 1.0, 0.0))
        step = half * rest
        for _ in range(5):
            step = half * (rest - exact_dot(step.T, step))
        unit = eye.astype(jnp.float32)
        inverse = unit - step
        whole = unit + step
        for _ in range(2):
            inverse = exact_dot(inverse, 2.0 * unit - exact_dot(whole, inverse))
        out_ref[...] = inverse

    @pl.when(jnp.logical_not(size < 0.01))
    def _():
        _, small = eliminate(eye.astype(jnp.float32) + rest, a_ref, b_ref)
        out_ref[...] = small.T

    basis_ref[...] = scale * exact_dot(above, out_ref[...])


def local_gram(range_columns):
    width = range_columns.shape[0]
    return pl.pallas_call(
        gram_kernel,
        out_shape=jax.ShapeDtypeStruct((2, width // 2 + 16, width), jnp.float32),
        name="local_gram",
    )(range_columns)


def two_factors(pair, total_snps):
    width = pair.shape[2]
    return pl.pallas_call(
        functools.partial(factor_kernel, math.sqrt(total_snps), float(total_snps)),
        out_shape=(
            jax.ShapeDtypeStruct((width, width), jnp.float32),
            jax.ShapeDtypeStruct((1, width), jnp.float32),
        ),
        scratch_shapes=[pltpu.VMEM((width, width), jnp.float32)] * 3,
        name="two_factors",
    )(pair)


STEPS = 3


def stats_kernel(samples, dosage_ref, out_ref, first_ref, square_ref):
    step = pl.program_id(0)

    @pl.when(step == 0)
    def _():
        first_ref[...] = jnp.zeros_like(first_ref)
        square_ref[...] = jnp.zeros_like(square_ref)

    values = dosage_ref[...].astype(jnp.float32)
    values = values.reshape(values.shape[0] // 8, 8, values.shape[1])
    first_ref[...] += jnp.sum(values, axis=0)
    square_ref[...] += jnp.sum(values * values, axis=0)

    @pl.when(step == pl.num_programs(0) - 1)
    def _():
        first = jnp.sum(first_ref[...], axis=0, keepdims=True)
        square = jnp.sum(square_ref[...], axis=0, keepdims=True)
        whole = first.astype(jnp.int32)
        exact = samples * square.astype(jnp.int32) - whole * whole
        spread = exact.astype(jnp.float32) / float(samples * samples)
        out_ref[0:1] = first / float(samples)
        out_ref[1:2] = lax.rsqrt(jnp.sqrt(jnp.sqrt(spread + 1e-05)))


def dosage_stats(genotypes):
    samples, width = genotypes.shape
    return pl.pallas_call(
        functools.partial(stats_kernel, samples),
        grid=(8,),
        in_specs=[pl.BlockSpec((samples // 8, width), lambda i: (i, 0))],
        out_specs=pl.BlockSpec((2, width), lambda i: (0, 0)),
        out_shape=jax.ShapeDtypeStruct((2, width), jnp.float32),
        scratch_shapes=[pltpu.VMEM((8, width), jnp.float32)] * 2,
        name="dosage_stats",
    )(genotypes)


def scaled_block(dosage_ref, stats_ref):
    centered = dosage_ref[...].astype(jnp.float32) - stats_ref[0:1]
    return (centered * stats_ref[1:2]).astype(jnp.bfloat16)


def sketch_kernel(table_ref, keep_ref, give_ref, stats_ref, probes_ref, kept_ref, given_ref):
    for source, target in ((give_ref, given_ref), (keep_ref, kept_ref)):
        target[...] = jnp.dot(
            scaled_block(source, stats_ref), probes_ref[...], preferred_element_type=jnp.float32
        )


def row_specs(k, rows, width):
    def keep(i, table):
        return table[k] * STEPS + i, 0

    def give(i, table):
        return table[4 + k] * STEPS + i, 0

    return [pl.BlockSpec((rows, width), keep), pl.BlockSpec((rows, width), give)]


def fixed(shape):
    return pl.BlockSpec(shape, lambda i, table: (0, 0))


def moving(shape):
    return pl.BlockSpec(shape, lambda i, table: (i, 0))


def sketch_piece(k, table, genotypes, stats, probes):
    samples, snps = genotypes.shape
    width = probes.shape[1]
    rows = samples // 8 // STEPS
    return pl.pallas_call(
        sketch_kernel,
        grid_spec=pltpu.PrefetchScalarGridSpec(
            num_scalar_prefetch=1,
            grid=(STEPS,),
            in_specs=[*row_specs(k, rows, snps), fixed((2, snps)), fixed((snps, width))],
            out_specs=[moving((rows, width))] * 2,
        ),
        out_shape=[jax.ShapeDtypeStruct((samples // 8, width), jnp.float32)] * 2,
        cost_estimate=pl.CostEstimate(
            flops=samples // 2 * snps * width, transcendentals=0, bytes_accessed=samples * snps // 2
        ),
        name="sketch_piece",
    )(table, genotypes, genotypes, stats, probes)


def range_kernel(table_ref, keep_ref, give_ref, stats_ref, mine_ref, theirs_ref, acc_ref, out_ref):
    width = acc_ref.shape[0]

    @pl.when(pl.program_id(0) == 0)
    def _():
        out_ref[...] = acc_ref[...]

    for dosage_ref, sketch_ref in ((keep_ref, mine_ref), (give_ref, theirs_ref)):
        sketch = sketch_ref[...].T
        high = sketch.astype(jnp.bfloat16)
        rest = sketch - high.astype(jnp.float32)
        mid = rest.astype(jnp.bfloat16)
        low = (rest - mid.astype(jnp.float32)).astype(jnp.bfloat16)
        parts = jnp.concatenate([high, mid, low], axis=0)
        product = jnp.dot(
            parts, scaled_block(dosage_ref, stats_ref), preferred_element_type=jnp.float32
        )
        out_ref[...] += product[:width] + product[width : 2 * width] + product[2 * width :]


def range_piece(k, table, genotypes, stats, mine, theirs, acc):
    samples, snps = genotypes.shape
    width = mine.shape[1]
    rows = samples // 8 // STEPS
    return pl.pallas_call(
        range_kernel,
        grid_spec=pltpu.PrefetchScalarGridSpec(
            num_scalar_prefetch=1,
            grid=(STEPS,),
            in_specs=[
                *row_specs((4 - k) % 4, rows, snps),
                fixed((2, snps)),
                moving((rows, width)),
                moving((rows, width)),
                fixed((width, snps)),
            ],
            out_specs=fixed((width, snps)),
        ),
        out_shape=jax.ShapeDtypeStruct((width, snps), jnp.float32),
        cost_estimate=pl.CostEstimate(
            flops=3 * samples // 2 * snps * width, transcendentals=0, bytes_accessed=samples * snps // 2
        ),
        name="range_piece",
    )(table, genotypes, genotypes, stats, mine, theirs, acc)


def solution(mesh):
    nx = mesh.shape["chrom"]
    nz = mesh.shape["snp"] // 8
    torus = Torus((nx, nz, 4, 2))
    fine = Mesh(mesh.devices.reshape(torus.sizes), AXES)

    def body(genotypes, probes):
        samples, snps = genotypes.shape
        width = probes.shape[1]
        total_snps = snps * fine.size
        core, one, two = torus.places()
        turns = jnp.arange(4, dtype=jnp.int32)
        table = jnp.concatenate(
            [core * 4 + (one + turns) % 4, (1 - core) * 4 + (two + turns) % 4]
        ).astype(jnp.int32)
        stats = dosage_stats(genotypes)
        got = {}
        for k in (2, 1, 3, 0):
            kept, given = sketch_piece(k, table, genotypes, stats, probes)
            piece = kept + torus.core(given)
            got[k] = torus.first(piece, k) if k else piece
        quarter = (got[0] + got[2]) + (got[1] + got[3])
        small = scatter_ring(quarter.reshape(4, samples // 32, width), two, torus.second)
        small = small.reshape(nz, samples // 32 // nz, width)
        own = lax.all_to_all(small, "z", 0, 0).sum(0)
        small = lax.all_to_all(jnp.broadcast_to(own, (nz, *own.shape)), "z", 0, 0)
        quarter = gather_ring(small.reshape(samples // 32, width), two, torus.second)
        quarter = quarter.reshape(samples // 8, width)
        mine = {0: quarter}
        for k in (1, 3, 2):
            mine[k] = torus.first(quarter, k)
        acc = jnp.zeros((width, snps), jnp.float32)
        for k in (0, 1, 3, 2):
            theirs = torus.core(mine[k])
            acc = range_piece(k, table, genotypes, stats, mine[k], theirs, acc)
        pair = sum_square(torus, local_gram(acc))
        basis, range_log_norms = two_factors(pair, total_snps)
        unit_basis = lax.dot_general(
            acc,
            basis,
            (((0,), (0,)), ((), ())),
            precision=lax.Precision.HIGHEST,
            preferred_element_type=jnp.float32,
        )
        return (unit_basis, range_log_norms[0])

    return jax.shard_map(
        body,
        mesh=fine,
        in_specs=(P(None, AXES), P(AXES, None)),
        out_specs=(P(AXES, None), P()),
        check_vma=False,
    )
```

```python
import functools
import math

import jax
import jax.numpy as jnp
from jax import lax
from jax.experimental import pallas as pl
from jax.experimental.pallas import tpu as pltpu
from jax.sharding import Mesh
from jax.sharding import PartitionSpec as P


AXES = ("x", "z", "y", "c")


def pair_list(sizes, move):
    nx, nz, ny, nc = sizes
    pairs = []
    for x in range(nx):
        for z in range(nz):
            for y in range(ny):
                for c in range(nc):
                    X, Z, Y, C = move(x, z, y, c)
                    src = ((x * nz + z) * ny + y) * nc + c
                    dst = (((X % nx) * nz + Z % nz) * ny + Y % ny) * nc + C % nc
                    pairs.append((src, dst))
    return pairs


class Torus:
    def __init__(self, sizes):
        self.sizes = sizes

    def core(self, value):
        return lax.ppermute(value, AXES, pair_list(self.sizes, lambda x, z, y, c: (x, z, y, c + 1)))

    def first(self, value, k):
        def move(x, z, y, c):
            return (x + k, z, y, c) if c == 0 else (x, z, y + k, c)

        return lax.ppermute(value, AXES, pair_list(self.sizes, move))

    def second(self, value, k):
        def move(x, z, y, c):
            return (x, z, y + k, c) if c == 0 else (x + k, z, y, c)

        return lax.ppermute(value, AXES, pair_list(self.sizes, move))

    def places(self):
        core, x, y = lax.axis_index("c"), lax.axis_index("x"), lax.axis_index("y")
        return core, jnp.where(core == 0, x, y), jnp.where(core == 0, y, x)


def add_pairs(a, b):
    total = a[0] + b[0]
    back = total - a[0]
    lost = (a[0] - (total - back)) + (b[0] - back)
    return jnp.stack([total, (a[1] + b[1]) + lost])


def sum_ring(value, send):
    got = [send(value, k) for k in (1, 2, 3)]
    return add_pairs(add_pairs(value, got[1]), add_pairs(got[0], got[2]))


def tree_sum(terms, add):
    while len(terms) > 1:
        terms = [add(*terms[i : i + 2]) for i in range(0, len(terms), 2)]
    return terms[0]


def sum_square(torus, kept, given):
    half = add_pairs(kept, torus.core(given))
    half = sum_ring(half, torus.first)
    half = sum_ring(half, torus.second)
    depth = torus.sizes[1]
    got = lax.all_to_all(jnp.broadcast_to(half, (depth, *half.shape)), "z", 0, 0)
    half = tree_sum([got[i] for i in range(depth)], add_pairs)
    return half, torus.core(half)


LIMIT = pltpu.CompilerParams(vmem_limit_bytes=20 * 2**20)
ONCHIP = pl.BlockSpec(memory_space=pltpu.VMEM)
SCALARS = pl.BlockSpec(memory_space=pltpu.SMEM)
SLICES = 5


def cut(values, peak):
    sigma = peak * 131072.0
    slices = []
    for _ in range(SLICES):
        part = (values + sigma) - sigma
        slices.append(part.astype(jnp.bfloat16))
        values = values - part
        sigma = sigma * 0.0078125
    return slices


def exact_gram(values):
    flipped = values.T
    right = cut(values, jnp.max(jnp.abs(values), axis=0, keepdims=True))
    left = cut(flipped, jnp.max(jnp.abs(flipped), axis=1, keepdims=True))
    hi = jnp.zeros((values.shape[1], values.shape[1]), jnp.float32)
    lo = jnp.zeros_like(hi)
    for level in reversed(range(SLICES + 1)):
        for i in range(SLICES):
            if 0 <= level - i < SLICES:
                term = jnp.dot(left[i], right[level - i], preferred_element_type=jnp.float32)
                total = hi + term
                back = total - hi
                lo = lo + ((hi - (total - back)) + (term - back))
                hi = total
    return hi, lo


def pack(square):
    n = square.shape[0]
    row = lax.broadcasted_iota(jnp.int32, (n // 2, n), 0)
    col = lax.broadcasted_iota(jnp.int32, (n // 2, n), 1)
    last = pltpu.roll(square[n // 2 :], n // 2, 1)
    diagonal = jnp.sum(jnp.where(col == row, last, 0.0), axis=0, keepdims=True)
    tail = jnp.where(lax.broadcasted_iota(jnp.int32, (16, n), 0) == 0, diagonal, 0.0)
    return jnp.concatenate([jnp.where(col >= row, square[: n // 2], last), tail], axis=0)


def unpack(packed):
    n = packed.shape[1]
    row = lax.broadcasted_iota(jnp.int32, (n, n), 0)
    col = lax.broadcasted_iota(jnp.int32, (n, n), 1)
    diagonal = pltpu.roll(packed[n // 2 : n // 2 + 8], n // 2, 1)[0:1]
    whole = jnp.concatenate([packed[: n // 2], jnp.zeros((n // 2, n), jnp.float32)], axis=0)
    flipped = whole.T
    low = pltpu.roll(pltpu.roll(whole, n // 2, 0), n // 2, 1)
    low_flipped = pltpu.roll(pltpu.roll(flipped, n // 2, 0), n // 2, 1)
    last = jnp.where(col < row, low, jnp.where(col == row, diagonal, low_flipped))
    below = jnp.where(col < n // 2, flipped, last)
    return jnp.where(row < n // 2, jnp.where(col >= row, whole, flipped), below)


def gram_kernel(table_ref, range_ref, kept_ref, given_ref):
    rows = kept_ref.shape[1]
    first = table_ref[12] == 0
    for i, square in enumerate(exact_gram(range_ref[...].T)):
        packed = pack(square)
        kept_ref[i] = jnp.where(first, packed[:rows], packed[rows:])
        given_ref[i] = jnp.where(first, packed[rows:], packed[:rows])


def exact_dot(a, b):
    return lax.dot_general(
        a,
        b,
        (((1,), (0,)), ((), ())),
        precision=lax.Precision.HIGHEST,
        preferred_element_type=jnp.float32,
    )


def eliminate(matrix, a_ref, b_ref):
    n = matrix.shape[0]
    row = lax.broadcasted_iota(jnp.int32, (n, n), 0)
    col = lax.broadcasted_iota(jnp.int32, (n, n), 1)
    a_ref[...] = matrix
    b_ref[...] = (row == col).astype(jnp.float32)
    column_row = lax.broadcasted_iota(jnp.int32, (n, 1), 0)
    panel_row = lax.broadcasted_iota(jnp.int32, (8, 1), 0)

    def block(index, carry):
        start = pl.multiple_of(index * 8, 8)
        a, b = a_ref[...], b_ref[...]
        pa, pb = a_ref[pl.ds(start, 8), :], b_ref[pl.ds(start, 8), :]
        for t in range(8):
            inverse = 1.0 / pa[t : t + 1, t : t + 1]
            ra, rb = pa[t : t + 1, :] * inverse, pb[t : t + 1, :] * inverse
            factor = jnp.where(column_row > start + t, a[:, t : t + 1], 0.0)
            a, b = a - factor * ra, b - factor * rb
            if t < 7:
                factor = jnp.where(panel_row > t, pa[:, t : t + 1], 0.0)
                pa, pb = pa - factor * ra, pb - factor * rb
        a_ref[...] = pltpu.roll(a, n - 8, 1)
        b_ref[...] = b
        return carry

    lax.fori_loop(0, n // 8, block, 0)
    upper = jnp.where(col >= row, a_ref[...], 0.0)
    pivot = jnp.sum(jnp.where(col == row, upper, 0.0), axis=1, keepdims=True)
    root = lax.rsqrt(pivot)
    return upper * root, b_ref[...] * root


def factor_kernel(scale, count, table_ref, half_ref, other_ref, basis_ref, norms_ref, a_ref, b_ref, out_ref):
    first = table_ref[12] == 0
    squares = []
    for i in range(2):
        above = jnp.where(first, half_ref[i], other_ref[i])
        below = jnp.where(first, other_ref[i], half_ref[i])
        squares.append(unpack(jnp.concatenate([above, below], axis=0)))
    hi, lo = squares
    n = hi.shape[0]
    row = lax.broadcasted_iota(jnp.int32, (n, n), 0)
    col = lax.broadcasted_iota(jnp.int32, (n, n), 1)
    eye = row == col
    total = hi + lo
    lo = (hi - total) + lo
    hi = total
    diagonal = jnp.sum(jnp.where(eye, hi, 0.0), axis=0, keepdims=True)
    norms_ref[...] = 0.1 * jnp.log(diagonal / count)
    upper, below = eliminate(hi, a_ref, b_ref)
    back_hi, back_lo = exact_gram(upper)
    rest = ((hi - back_hi) - back_lo) + lo
    above = below.T
    rest = exact_dot(exact_dot(below, rest), above)
    size = jnp.sum(rest * rest)

    @pl.when(size < 0.01)
    def _():
        half = jnp.where(eye, 0.5, jnp.where(col > row, 1.0, 0.0))
        step = half * rest
        for _ in range(5):
            step = half * (rest - exact_dot(step.T, step))
        unit = eye.astype(jnp.float32)
        inverse = unit - step
        whole = unit + step
        for _ in range(2):
            inverse = exact_dot(inverse, 2.0 * unit - exact_dot(whole, inverse))
        out_ref[...] = inverse

    @pl.when(jnp.logical_not(size < 0.01))
    def _():
        _, small = eliminate(eye.astype(jnp.float32) + rest, a_ref, b_ref)
        out_ref[...] = small.T

    basis_ref[...] = scale * exact_dot(above, out_ref[...])


def local_gram(table, range_columns):
    width = range_columns.shape[0]
    return pl.pallas_call(
        gram_kernel,
        in_specs=[SCALARS, ONCHIP],
        out_specs=[ONCHIP] * 2,
        out_shape=[jax.ShapeDtypeStruct((2, width // 4 + 8, width), jnp.float32)] * 2,
        compiler_params=LIMIT,
        name="local_gram",
    )(table, range_columns)


def two_factors(table, half, other, total_snps):
    width = half.shape[2]
    return pl.pallas_call(
        functools.partial(factor_kernel, math.sqrt(total_snps), float(total_snps)),
        in_specs=[SCALARS] + [ONCHIP] * 2,
        out_shape=(
            jax.ShapeDtypeStruct((width, width), jnp.float32),
            jax.ShapeDtypeStruct((1, width), jnp.float32),
        ),
        scratch_shapes=[pltpu.VMEM((width, width), jnp.float32)] * 3,
        compiler_params=LIMIT,
        name="two_factors",
    )(table, half, other)


STEPS = 3
CHUNKS = 16


def resident(shape, dtype=jnp.float32):
    return pltpu.VMEM(shape, dtype)


def onchip(value):
    return pltpu.with_memory_space_constraint(value, pltpu.VMEM)


def offchip(value):
    return pltpu.with_memory_space_constraint(value, pltpu.HBM)


def stats_kernel(table_ref, source_ref, held_ref, out_ref, sems):
    samples, width = source_ref.shape
    rows = samples // CHUNKS

    def copy(i):
        part = pl.ds(pl.multiple_of(i * rows, rows), rows)
        return pltpu.make_async_copy(source_ref.at[part], held_ref.at[part], sems.at[i])

    for i in range(CHUNKS):
        copy(i).start()

    def add(i, sums):
        copy(i).wait()
        values = held_ref[pl.ds(pl.multiple_of(i * rows, rows), rows), :].astype(jnp.float32)
        values = values.reshape(rows // 8, 8, width)
        return sums[0] + jnp.sum(values, axis=0), sums[1] + jnp.sum(values * values, axis=0)

    zero = jnp.zeros((8, width), jnp.float32)
    first, square = lax.fori_loop(0, CHUNKS, add, (zero, zero))
    first = jnp.sum(first, axis=0, keepdims=True)
    square = jnp.sum(square, axis=0, keepdims=True)
    whole = first.astype(jnp.int32)
    exact = samples * square.astype(jnp.int32) - whole * whole
    spread = exact.astype(jnp.float32) / float(samples * samples)
    out_ref[0:1] = first / float(samples)
    out_ref[1:2] = lax.rsqrt(jnp.sqrt(jnp.sqrt(spread + 1e-05)))


def dosage_stats(table, genotypes):
    samples, width = genotypes.shape
    return pl.pallas_call(
        stats_kernel,
        in_specs=[SCALARS, pl.BlockSpec(memory_space=pltpu.HBM)],
        out_specs=[ONCHIP] * 2,
        out_shape=[resident((samples, width), genotypes.dtype), resident((2, width))],
        scratch_shapes=[pltpu.SemaphoreType.DMA((CHUNKS,))],
        compiler_params=LIMIT,
        name="dosage_stats",
    )(table, offchip(genotypes))


def scaled_rows(held_ref, stats_ref, start, rows):
    dosages = held_ref[pl.ds(pl.multiple_of(start, rows), rows), :].astype(jnp.float32)
    return ((dosages - stats_ref[0:1]) * stats_ref[1:2]).astype(jnp.bfloat16)


def sum_kernel(table_ref, zero_ref, one_ref, two_ref, three_ref, *out_refs):
    rows = out_refs[0].shape[0]
    for k, out_ref in enumerate(out_refs):
        part = pl.ds(pl.multiple_of(table_ref[8 + k] * rows, rows), rows)
        out_ref[...] = (zero_ref[part] + two_ref[part]) + (one_ref[part] + three_ref[part])


def sum_quarter(table, got):
    rows, width = got[0].shape
    return pl.pallas_call(
        sum_kernel,
        in_specs=[SCALARS] + [ONCHIP] * 4,
        out_specs=[ONCHIP] * 4,
        out_shape=[resident((rows // 4, width))] * 4,
        compiler_params=LIMIT,
        name="sum_quarter",
    )(table, *(onchip(got[k]) for k in range(4)))


def join_kernel(table_ref, *refs):
    *part_refs, out_ref = refs
    rows = part_refs[0].shape[0]
    for k, part_ref in enumerate(part_refs):
        start = pl.multiple_of(table_ref[8 + (4 - k) % 4] * rows, rows)
        out_ref[pl.ds(start, rows)] = part_ref[...]


def join_quarter(table, parts):
    rows, width = parts[0].shape
    return pl.pallas_call(
        join_kernel,
        in_specs=[SCALARS] + [ONCHIP] * 4,
        out_specs=ONCHIP,
        out_shape=resident((4 * rows, width)),
        compiler_params=LIMIT,
        name="join_quarter",
    )(table, *(onchip(part) for part in parts))


def sketch_kernel(k, table_ref, held_ref, stats_ref, probes_ref, kept_ref, given_ref):
    whole = kept_ref.shape[0]
    rows = whole // STEPS

    def step(i, carry):
        part = pl.ds(pl.multiple_of(i * rows, rows), rows)
        for slot, target in ((4 + k, given_ref), (k, kept_ref)):
            scaled = scaled_rows(held_ref, stats_ref, table_ref[slot] * whole + i * rows, rows)
            target[part, :] = jnp.dot(scaled, probes_ref[...], preferred_element_type=jnp.float32)
        return carry

    lax.fori_loop(0, STEPS, step, 0)


def sketch_piece(k, table, held, stats, probes):
    samples, snps = held.shape
    width = probes.shape[1]
    return pl.pallas_call(
        functools.partial(sketch_kernel, k),
        in_specs=[SCALARS, ONCHIP, ONCHIP, ONCHIP],
        out_specs=[ONCHIP] * 2,
        out_shape=[resident((samples // 8, width))] * 2,
        compiler_params=LIMIT,
        cost_estimate=pl.CostEstimate(
            flops=samples // 2 * snps * width, transcendentals=0, bytes_accessed=samples * snps // 2
        ),
        name="sketch_piece",
    )(table, held, stats, probes)


def range_kernel(k, table_ref, held_ref, stats_ref, mine_ref, theirs_ref, acc_ref, out_ref):
    width = acc_ref.shape[0]
    whole = mine_ref.shape[0]
    rows = whole // STEPS
    out_ref[...] = acc_ref[...]

    def step(i, carry):
        part = pl.ds(pl.multiple_of(i * rows, rows), rows)
        for slot, sketch_ref in ((k, mine_ref), (4 + k, theirs_ref)):
            sketch = sketch_ref[part, :].T
            high = sketch.astype(jnp.bfloat16)
            rest = sketch - high.astype(jnp.float32)
            mid = rest.astype(jnp.bfloat16)
            low = (rest - mid.astype(jnp.float32)).astype(jnp.bfloat16)
            parts = jnp.concatenate([high, mid, low], axis=0)
            scaled = scaled_rows(held_ref, stats_ref, table_ref[slot] * whole + i * rows, rows)
            product = jnp.dot(parts, scaled, preferred_element_type=jnp.float32)
            out_ref[...] += product[:width] + product[width : 2 * width] + product[2 * width :]
        return carry

    lax.fori_loop(0, STEPS, step, 0)


def range_piece(k, table, held, stats, mine, theirs, acc):
    samples, snps = held.shape
    width = mine.shape[1]
    return pl.pallas_call(
        functools.partial(range_kernel, (4 - k) % 4),
        in_specs=[SCALARS] + [ONCHIP] * 5,
        out_specs=ONCHIP,
        out_shape=resident((width, snps)),
        compiler_params=LIMIT,
        cost_estimate=pl.CostEstimate(
            flops=3 * samples // 2 * snps * width, transcendentals=0, bytes_accessed=samples * snps // 2
        ),
        name="range_piece",
    )(table, held, stats, onchip(mine), onchip(theirs), acc)


def solution(mesh):
    nx = mesh.shape["chrom"]
    nz = mesh.shape["snp"] // 8
    torus = Torus((nx, nz, 4, 2))
    fine = Mesh(mesh.devices.reshape(torus.sizes), AXES)

    def body(genotypes, probes):
        samples, snps = genotypes.shape
        width = probes.shape[1]
        total_snps = snps * fine.size
        core, one, two = torus.places()
        turns = jnp.arange(4, dtype=jnp.int32)
        table = jnp.concatenate(
            [
                core * 4 + ((one + turns) & 3),
                (1 - core) * 4 + ((two + turns) & 3),
                (two + turns) & 3,
                core[None],
            ]
        ).astype(jnp.int32)
        held, stats = (onchip(v) for v in dosage_stats(table, genotypes))
        got = {}
        for k in (2, 1, 3, 0):
            kept, given = sketch_piece(k, table, held, stats, probes)
            piece = kept + torus.core(given)
            got[k] = torus.first(piece, k) if k else piece
        split = sum_quarter(table, got)
        got = [torus.second(split[k], k) for k in (1, 2, 3)]
        small = (split[0] + got[1]) + (got[0] + got[2])
        small = small.reshape(nz, samples // 32 // nz, width)
        own = lax.all_to_all(small, "z", 0, 0)
        own = tree_sum([own[i] for i in range(nz)], jnp.add)
        small = lax.all_to_all(jnp.broadcast_to(own, (nz, *own.shape)), "z", 0, 0)
        small = small.reshape(samples // 32, width)
        quarter = join_quarter(table, [small] + [torus.second(small, k) for k in (1, 2, 3)])
        mine = {0: quarter}
        for k in (1, 3, 2):
            mine[k] = torus.first(quarter, k)
        acc = jnp.zeros((width, snps), jnp.float32)
        for k in (0, 1, 3, 2):
            theirs = torus.core(mine[k])
            acc = range_piece(k, table, held, stats, mine[k], theirs, acc)
        half, other = sum_square(torus, *local_gram(table, acc))
        basis, range_log_norms = two_factors(table, half, other, total_snps)
        unit_basis = lax.dot_general(
            acc,
            basis,
            (((0,), (0,)), ((), ())),
            precision=lax.Precision.HIGHEST,
            preferred_element_type=jnp.float32,
        )
        return (unit_basis, range_log_norms[0])

    return jax.shard_map(
        body,
        mesh=fine,
        in_specs=(P(None, AXES), P(AXES, None)),
        out_specs=(P(AXES, None), P()),
        check_vma=False,
    )
```

```python
import functools
import math

import jax
import jax.numpy as jnp
from jax import lax
from jax.experimental import pallas as pl
from jax.experimental.pallas import tpu as pltpu
from jax.sharding import Mesh
from jax.sharding import PartitionSpec as P


AXES = ("x", "z", "y", "c")


def pair_list(sizes, move):
    nx, nz, ny, nc = sizes
    pairs = []
    for x in range(nx):
        for z in range(nz):
            for y in range(ny):
                for c in range(nc):
                    X, Z, Y, C = move(x, z, y, c)
                    src = ((x * nz + z) * ny + y) * nc + c
                    dst = (((X % nx) * nz + Z % nz) * ny + Y % ny) * nc + C % nc
                    pairs.append((src, dst))
    return pairs


class Torus:
    def __init__(self, sizes):
        self.sizes = sizes

    def core(self, value):
        return lax.ppermute(value, AXES, pair_list(self.sizes, lambda x, z, y, c: (x, z, y, c + 1)))

    def first(self, value, k):
        def move(x, z, y, c):
            return (x + k, z, y, c) if c == 0 else (x, z, y + k, c)

        return lax.ppermute(value, AXES, pair_list(self.sizes, move))

    def second(self, value, k):
        def move(x, z, y, c):
            return (x, z, y + k, c) if c == 0 else (x + k, z, y, c)

        return lax.ppermute(value, AXES, pair_list(self.sizes, move))

    def places(self):
        core, x, y = lax.axis_index("c"), lax.axis_index("x"), lax.axis_index("y")
        return core, jnp.where(core == 0, x, y), jnp.where(core == 0, y, x)


def add_pairs(a, b):
    total = a[0] + b[0]
    back = total - a[0]
    lost = (a[0] - (total - back)) + (b[0] - back)
    return jnp.stack([total, (a[1] + b[1]) + lost])


def sum_ring(value, send):
    got = [send(value, k) for k in (1, 2, 3)]
    return add_pairs(add_pairs(value, got[1]), add_pairs(got[0], got[2]))


def tree_sum(terms, add):
    while len(terms) > 1:
        terms = [add(*terms[i : i + 2]) for i in range(0, len(terms), 2)]
    return terms[0]


def sum_square(torus, kept, given):
    half = add_pairs(kept, torus.core(given))
    half = sum_ring(half, torus.first)
    half = sum_ring(half, torus.second)
    depth = torus.sizes[1]
    got = lax.all_to_all(jnp.broadcast_to(half, (depth, *half.shape)), "z", 0, 0)
    half = tree_sum([got[i] for i in range(depth)], add_pairs)
    return half, torus.core(half)


LIMIT = pltpu.CompilerParams(vmem_limit_bytes=20 * 2**20)
ONCHIP = pl.BlockSpec(memory_space=pltpu.VMEM)
SCALARS = pl.BlockSpec(memory_space=pltpu.SMEM)
SLICES = 5


def cut(values, peak):
    sigma = peak * 131072.0
    slices = []
    for _ in range(SLICES):
        part = (values + sigma) - sigma
        slices.append(part.astype(jnp.bfloat16))
        values = values - part
        sigma = sigma * 0.0078125
    return slices


def exact_gram(values, joined):
    flipped = values.T
    right = cut(values, jnp.max(jnp.abs(values), axis=0, keepdims=True))
    left = cut(flipped, jnp.max(jnp.abs(flipped), axis=1, keepdims=True))
    hi = jnp.zeros((values.shape[1], values.shape[1]), jnp.float32)
    lo = jnp.zeros_like(hi)
    for level in reversed(range(SLICES + 1)):
        picks = [i for i in range(SLICES) if 0 <= level - i < SLICES]
        for group in [picks] if joined else [[i] for i in picks]:
            term = jnp.dot(
                jnp.concatenate([left[i] for i in group], axis=1),
                jnp.concatenate([right[level - i] for i in group], axis=0),
                preferred_element_type=jnp.float32,
            )
            total = hi + term
            back = total - hi
            lo = lo + ((hi - (total - back)) + (term - back))
            hi = total
    return hi, lo


def pack(square):
    n = square.shape[0]
    row = lax.broadcasted_iota(jnp.int32, (n // 2, n), 0)
    col = lax.broadcasted_iota(jnp.int32, (n // 2, n), 1)
    last = pltpu.roll(square[n // 2 :], n // 2, 1)
    diagonal = jnp.sum(jnp.where(col == row, last, 0.0), axis=0, keepdims=True)
    tail = jnp.where(lax.broadcasted_iota(jnp.int32, (16, n), 0) == 0, diagonal, 0.0)
    return jnp.concatenate([jnp.where(col >= row, square[: n // 2], last), tail], axis=0)


def unpack(packed):
    n = packed.shape[1]
    row = lax.broadcasted_iota(jnp.int32, (n, n), 0)
    col = lax.broadcasted_iota(jnp.int32, (n, n), 1)
    diagonal = pltpu.roll(packed[n // 2 : n // 2 + 8], n // 2, 1)[0:1]
    whole = jnp.concatenate([packed[: n // 2], jnp.zeros((n // 2, n), jnp.float32)], axis=0)
    flipped = whole.T
    low = pltpu.roll(pltpu.roll(whole, n // 2, 0), n // 2, 1)
    low_flipped = pltpu.roll(pltpu.roll(flipped, n // 2, 0), n // 2, 1)
    last = jnp.where(col < row, low, jnp.where(col == row, diagonal, low_flipped))
    below = jnp.where(col < n // 2, flipped, last)
    return jnp.where(row < n // 2, jnp.where(col >= row, whole, flipped), below)


def gram_kernel(table_ref, range_ref, kept_ref, given_ref):
    rows = kept_ref.shape[1]
    first = table_ref[12] == 0
    for i, square in enumerate(exact_gram(range_ref[...].T, False)):
        packed = pack(square)
        kept_ref[i] = jnp.where(first, packed[:rows], packed[rows:])
        given_ref[i] = jnp.where(first, packed[rows:], packed[:rows])


def exact_dot(a, b):
    return lax.dot_general(
        a,
        b,
        (((1,), (0,)), ((), ())),
        precision=lax.Precision.HIGHEST,
        preferred_element_type=jnp.float32,
    )


def short_dot(a, b):
    a, b = a.astype(jnp.bfloat16), b.astype(jnp.bfloat16)
    return jnp.dot(a, b, preferred_element_type=jnp.float32)


def eliminate(matrix, a_ref, b_ref):
    n = matrix.shape[0]
    row = lax.broadcasted_iota(jnp.int32, (n, n), 0)
    col = lax.broadcasted_iota(jnp.int32, (n, n), 1)
    a_ref[...] = matrix
    b_ref[...] = (row == col).astype(jnp.float32)
    column_row = lax.broadcasted_iota(jnp.int32, (n, 1), 0)
    panel_row = lax.broadcasted_iota(jnp.int32, (8, 1), 0)

    def block(index, carry):
        start = pl.multiple_of(index * 8, 8)
        a, b = a_ref[...], b_ref[...]
        pa, pb = a_ref[pl.ds(start, 8), :], b_ref[pl.ds(start, 8), :]
        after = column_row >= start + 8
        for t in range(8):
            lane = jnp.broadcast_to(pa[:, t : t + 1], (8, n))
            inverse = 1.0 / lane[t : t + 1]
            ra, rb = pa[t : t + 1], pb[t : t + 1]
            if t < 7:
                masked = jnp.where(panel_row > t, lane, 0.0)
                pa, pb = pa - (masked * ra) * inverse, pb - (masked * rb) * inverse
            factor = jnp.where(after, a[:, t : t + 1], 0.0)
            a, b = a - (factor * ra) * inverse, b - factor * (rb * inverse)
        a_ref[...] = pltpu.roll(a, n - 8, 1)
        b_ref[...] = b
        a_ref[pl.ds(start, 8), :] = pltpu.roll(pa, n - 8, 1)
        b_ref[pl.ds(start, 8), :] = pb
        return carry

    lax.fori_loop(0, n // 8, block, 0)
    upper = jnp.where(col >= row, a_ref[...], 0.0)
    pivot = jnp.sum(jnp.where(col == row, upper, 0.0), axis=1, keepdims=True)
    root = lax.rsqrt(pivot)
    return upper * root, b_ref[...] * root


def factor_kernel(scale, count, table_ref, half_ref, other_ref, basis_ref, norms_ref, a_ref, b_ref, out_ref):
    first = table_ref[12] == 0
    squares = []
    for i in range(2):
        above = jnp.where(first, half_ref[i], other_ref[i])
        below = jnp.where(first, other_ref[i], half_ref[i])
        squares.append(unpack(jnp.concatenate([above, below], axis=0)))
    hi, lo = squares
    n = hi.shape[0]
    row = lax.broadcasted_iota(jnp.int32, (n, n), 0)
    col = lax.broadcasted_iota(jnp.int32, (n, n), 1)
    eye = row == col
    total = hi + lo
    lo = (hi - total) + lo
    hi = total
    diagonal = jnp.sum(jnp.where(eye, hi, 0.0), axis=0, keepdims=True)
    norms_ref[...] = 0.1 * jnp.log(diagonal / count)
    upper, below = eliminate(hi, a_ref, b_ref)
    back_hi, back_lo = exact_gram(upper, True)
    rest = ((hi - back_hi) - back_lo) + lo
    above = below.T
    rest = exact_dot(exact_dot(below, rest), above)
    size = jnp.sum(rest * rest)

    @pl.when(size < 0.002)
    def _():
        half = jnp.where(eye, 0.5, jnp.where(col > row, 1.0, 0.0))
        step = half * rest
        for _ in range(3):
            step = half * (rest - short_dot(step.T, step))
        square = short_dot(step, step)
        inverse = eye.astype(jnp.float32) - step
        inverse = inverse + short_dot(inverse, square)
        out_ref[...] = inverse + short_dot(inverse, short_dot(square, square))

    @pl.when(jnp.logical_not(size < 0.002))
    def _():
        _, small = eliminate(eye.astype(jnp.float32) + rest, a_ref, b_ref)
        out_ref[...] = small.T

    basis_ref[...] = scale * exact_dot(above, out_ref[...])


def local_gram(table, range_columns):
    width = range_columns.shape[0]
    return pl.pallas_call(
        gram_kernel,
        in_specs=[SCALARS, ONCHIP],
        out_specs=[ONCHIP] * 2,
        out_shape=[jax.ShapeDtypeStruct((2, width // 4 + 8, width), jnp.float32)] * 2,
        compiler_params=LIMIT,
        name="local_gram",
    )(table, range_columns)


def two_factors(table, half, other, total_snps):
    width = half.shape[2]
    return pl.pallas_call(
        functools.partial(factor_kernel, math.sqrt(total_snps), float(total_snps)),
        in_specs=[SCALARS] + [ONCHIP] * 2,
        out_shape=(
            jax.ShapeDtypeStruct((width, width), jnp.float32),
            jax.ShapeDtypeStruct((1, width), jnp.float32),
        ),
        scratch_shapes=[pltpu.VMEM((width, width), jnp.float32)] * 3,
        compiler_params=LIMIT,
        name="two_factors",
    )(table, half, other)


STEPS = 3
CHUNKS = 16


def resident(shape, dtype=jnp.float32):
    return pltpu.VMEM(shape, dtype)


def onchip(value):
    return pltpu.with_memory_space_constraint(value, pltpu.VMEM)


def offchip(value):
    return pltpu.with_memory_space_constraint(value, pltpu.HBM)


def stats_kernel(table_ref, source_ref, held_ref, out_ref, sems):
    samples, width = source_ref.shape
    rows = samples // CHUNKS

    def copy(i):
        part = pl.ds(pl.multiple_of(i * rows, rows), rows)
        return pltpu.make_async_copy(source_ref.at[part], held_ref.at[part], sems.at[i])

    for i in range(CHUNKS):
        copy(i).start()

    def add(i, sums):
        copy(i).wait()
        values = held_ref[pl.ds(pl.multiple_of(i * rows, rows), rows), :].astype(jnp.float32)
        values = values.reshape(rows // 8, 8, width)
        return sums[0] + jnp.sum(values, axis=0), sums[1] + jnp.sum(values * values, axis=0)

    zero = jnp.zeros((8, width), jnp.float32)
    first, square = lax.fori_loop(0, CHUNKS, add, (zero, zero))
    first = jnp.sum(first, axis=0, keepdims=True)
    square = jnp.sum(square, axis=0, keepdims=True)
    whole = first.astype(jnp.int32)
    exact = samples * square.astype(jnp.int32) - whole * whole
    spread = exact.astype(jnp.float32) / float(samples * samples)
    out_ref[0:1] = first / float(samples)
    out_ref[1:2] = lax.rsqrt(jnp.sqrt(jnp.sqrt(spread + 1e-05)))


def dosage_stats(table, genotypes):
    samples, width = genotypes.shape
    return pl.pallas_call(
        stats_kernel,
        in_specs=[SCALARS, pl.BlockSpec(memory_space=pltpu.HBM)],
        out_specs=[ONCHIP] * 2,
        out_shape=[resident((samples, width), genotypes.dtype), resident((2, width))],
        scratch_shapes=[pltpu.SemaphoreType.DMA((CHUNKS,))],
        compiler_params=LIMIT,
        name="dosage_stats",
    )(table, offchip(genotypes))


def scaled_rows(held_ref, stats_ref, start, rows):
    dosages = held_ref[pl.ds(pl.multiple_of(start, rows), rows), :].astype(jnp.float32)
    return ((dosages - stats_ref[0:1]) * stats_ref[1:2]).astype(jnp.bfloat16)


def sum_kernel(table_ref, zero_ref, one_ref, two_ref, three_ref, *out_refs):
    rows = out_refs[0].shape[0]
    for k, out_ref in enumerate(out_refs):
        part = pl.ds(pl.multiple_of(table_ref[8 + k] * rows, rows), rows)
        out_ref[...] = (zero_ref[part] + two_ref[part]) + (one_ref[part] + three_ref[part])


def sum_quarter(table, got):
    rows, width = got[0].shape
    return pl.pallas_call(
        sum_kernel,
        in_specs=[SCALARS] + [ONCHIP] * 4,
        out_specs=[ONCHIP] * 4,
        out_shape=[resident((rows // 4, width))] * 4,
        compiler_params=LIMIT,
        name="sum_quarter",
    )(table, *(onchip(got[k]) for k in range(4)))


def join_kernel(table_ref, *refs):
    *part_refs, out_ref = refs
    rows = part_refs[0].shape[0]
    for k, part_ref in enumerate(part_refs):
        start = pl.multiple_of(table_ref[8 + (4 - k) % 4] * rows, rows)
        out_ref[pl.ds(start, rows)] = part_ref[...]


def join_quarter(table, parts):
    rows, width = parts[0].shape
    return pl.pallas_call(
        join_kernel,
        in_specs=[SCALARS] + [ONCHIP] * 4,
        out_specs=ONCHIP,
        out_shape=resident((4 * rows, width)),
        compiler_params=LIMIT,
        name="join_quarter",
    )(table, *(onchip(part) for part in parts))


def sketch_kernel(k, table_ref, held_ref, stats_ref, probes_ref, kept_ref, given_ref):
    whole = kept_ref.shape[0]
    rows = whole // STEPS

    def step(i, carry):
        part = pl.ds(pl.multiple_of(i * rows, rows), rows)
        for slot, target in ((4 + k, given_ref), (k, kept_ref)):
            scaled = scaled_rows(held_ref, stats_ref, table_ref[slot] * whole + i * rows, rows)
            target[part, :] = jnp.dot(scaled, probes_ref[...], preferred_element_type=jnp.float32)
        return carry

    lax.fori_loop(0, STEPS, step, 0)


def sketch_piece(k, table, held, stats, probes):
    samples, snps = held.shape
    width = probes.shape[1]
    return pl.pallas_call(
        functools.partial(sketch_kernel, k),
        in_specs=[SCALARS, ONCHIP, ONCHIP, ONCHIP],
        out_specs=[ONCHIP] * 2,
        out_shape=[resident((samples // 8, width))] * 2,
        compiler_params=LIMIT,
        cost_estimate=pl.CostEstimate(
            flops=samples // 2 * snps * width, transcendentals=0, bytes_accessed=samples * snps // 2
        ),
        name="sketch_piece",
    )(table, held, stats, probes)


def range_kernel(slots, table_ref, held_ref, stats_ref, acc_ref, *refs):
    *sketch_refs, out_ref = refs
    width = acc_ref.shape[0]
    whole = sketch_refs[0].shape[0]
    rows = whole // STEPS
    out_ref[...] = acc_ref[...]

    def step(i, carry):
        part = pl.ds(pl.multiple_of(i * rows, rows), rows)
        for slot, sketch_ref in zip(slots, sketch_refs):
            sketch = sketch_ref[part, :].T
            high = sketch.astype(jnp.bfloat16)
            rest = sketch - high.astype(jnp.float32)
            mid = rest.astype(jnp.bfloat16)
            low = (rest - mid.astype(jnp.float32)).astype(jnp.bfloat16)
            parts = jnp.concatenate([high, mid, low], axis=0)
            scaled = scaled_rows(held_ref, stats_ref, table_ref[slot] * whole + i * rows, rows)
            product = jnp.dot(parts, scaled, preferred_element_type=jnp.float32)
            out_ref[...] += product[:width] + product[width : 2 * width] + product[2 * width :]
        return carry

    lax.fori_loop(0, STEPS, step, 0)


def range_piece(slots, table, held, stats, acc, *sketches):
    samples, snps = held.shape
    width = acc.shape[0]
    part = samples // 8 * len(slots)
    return pl.pallas_call(
        functools.partial(range_kernel, slots),
        in_specs=[SCALARS] + [ONCHIP] * (3 + len(slots)),
        out_specs=ONCHIP,
        out_shape=resident((width, snps)),
        compiler_params=LIMIT,
        cost_estimate=pl.CostEstimate(
            flops=6 * part * snps * width, transcendentals=0, bytes_accessed=2 * part * snps
        ),
        name="range_piece",
    )(table, held, stats, acc, *(onchip(sketch) for sketch in sketches))


def solution(mesh):
    nx = mesh.shape["chrom"]
    nz = mesh.shape["snp"] // 8
    torus = Torus((nx, nz, 4, 2))
    fine = Mesh(mesh.devices.reshape(torus.sizes), AXES)

    def body(genotypes, probes):
        samples, snps = genotypes.shape
        width = probes.shape[1]
        total_snps = snps * fine.size
        core, one, two = torus.places()
        turns = jnp.arange(4, dtype=jnp.int32)
        table = jnp.concatenate(
            [
                core * 4 + ((one + turns) & 3),
                (1 - core) * 4 + ((two + turns) & 3),
                (two + turns) & 3,
                core[None],
            ]
        ).astype(jnp.int32)
        held, stats = (onchip(v) for v in dosage_stats(table, genotypes))
        got = {}
        for k in (2, 1, 3, 0):
            kept, given = sketch_piece(k, table, held, stats, probes)
            piece = kept + torus.core(given)
            got[k] = torus.first(piece, k) if k else piece
        split = sum_quarter(table, got)
        got = [torus.second(split[k], k) for k in (1, 2, 3)]
        small = (split[0] + got[1]) + (got[0] + got[2])
        small = small.reshape(nz, samples // 32 // nz, width)
        own = lax.all_to_all(small, "z", 0, 0)
        own = tree_sum([own[i] for i in range(nz)], jnp.add)
        small = lax.all_to_all(jnp.broadcast_to(own, (nz, *own.shape)), "z", 0, 0)
        small = small.reshape(samples // 32, width)
        quarter = join_quarter(table, [small] + [torus.second(small, k) for k in (1, 2, 3)])
        mine = {0: quarter}
        for k in (1, 3, 2):
            mine[k] = torus.first(quarter, k)
        acc = jnp.zeros((width, snps), jnp.float32)
        acc = range_piece((0,), table, held, stats, acc, quarter)
        for k in (0, 1, 3, 2):
            slot = (4 - k) % 4
            theirs = torus.core(mine[k])
            if k:
                acc = range_piece((slot, 4 + slot), table, held, stats, acc, mine[k], theirs)
            else:
                acc = range_piece((4,), table, held, stats, acc, theirs)
        half, other = sum_square(torus, *local_gram(table, acc))
        basis, range_log_norms = two_factors(table, half, other, total_snps)
        unit_basis = lax.dot_general(
            acc,
            basis,
            (((0,), (0,)), ((), ())),
            precision=lax.Precision.HIGHEST,
            preferred_element_type=jnp.float32,
        )
        return (unit_basis, range_log_norms[0])

    return jax.shard_map(
        body,
        mesh=fine,
        in_specs=(P(None, AXES), P(AXES, None)),
        out_specs=(P(AXES, None), P()),
        check_vma=False,
    )
```

```python
import functools
import math

import jax
import jax.numpy as jnp
from jax import lax
from jax.experimental import pallas as pl
from jax.experimental.pallas import tpu as pltpu
from jax.sharding import Mesh
from jax.sharding import PartitionSpec as P


AXES = ("x", "z", "y", "c")


def pair_list(sizes, move):
    nx, nz, ny, nc = sizes
    pairs = []
    for x in range(nx):
        for z in range(nz):
            for y in range(ny):
                for c in range(nc):
                    X, Z, Y, C = move(x, z, y, c)
                    src = ((x * nz + z) * ny + y) * nc + c
                    dst = (((X % nx) * nz + Z % nz) * ny + Y % ny) * nc + C % nc
                    pairs.append((src, dst))
    return pairs


class Torus:
    def __init__(self, sizes):
        self.sizes = sizes

    def core(self, value):
        return lax.ppermute(value, AXES, pair_list(self.sizes, lambda x, z, y, c: (x, z, y, c + 1)))

    def first(self, value, k):
        def move(x, z, y, c):
            return (x + k, z, y, c) if c == 0 else (x, z, y + k, c)

        return lax.ppermute(value, AXES, pair_list(self.sizes, move))

    def second(self, value, k):
        def move(x, z, y, c):
            return (x, z, y + k, c) if c == 0 else (x + k, z, y, c)

        return lax.ppermute(value, AXES, pair_list(self.sizes, move))

    def places(self):
        core, x, y = lax.axis_index("c"), lax.axis_index("x"), lax.axis_index("y")
        return core, jnp.where(core == 0, x, y), jnp.where(core == 0, y, x)


def add_pairs(a, b):
    total = a[0] + b[0]
    back = total - a[0]
    lost = (a[0] - (total - back)) + (b[0] - back)
    return jnp.stack([total, (a[1] + b[1]) + lost])


def sum_ring(value, send):
    got = [send(value, k) for k in (1, 2, 3)]
    return add_pairs(add_pairs(value, got[1]), add_pairs(got[0], got[2]))


def tree_sum(terms, add):
    while len(terms) > 1:
        terms = [add(*terms[i : i + 2]) for i in range(0, len(terms), 2)]
    return terms[0]


def sum_square(torus, kept, given):
    half = add_pairs(kept, torus.core(given))
    half = sum_ring(half, torus.first)
    half = sum_ring(half, torus.second)
    depth = torus.sizes[1]
    got = lax.all_to_all(jnp.broadcast_to(half, (depth, *half.shape)), "z", 0, 0)
    half = tree_sum([got[i] for i in range(depth)], add_pairs)
    return half, torus.core(half)


LIMIT = pltpu.CompilerParams(vmem_limit_bytes=20 * 2**20)
ONCHIP = pl.BlockSpec(memory_space=pltpu.VMEM)
SCALARS = pl.BlockSpec(memory_space=pltpu.SMEM)
SLICES = 5


def cut(values, peak):
    sigma = peak * 131072.0
    slices = []
    for _ in range(SLICES):
        part = (values + sigma) - sigma
        slices.append(part.astype(jnp.bfloat16))
        values = values - part
        sigma = sigma * 0.0078125
    return slices


def exact_gram(values, joined):
    flipped = values.T
    right = cut(values, jnp.max(jnp.abs(values), axis=0, keepdims=True))
    left = cut(flipped, jnp.max(jnp.abs(flipped), axis=1, keepdims=True))
    hi = jnp.zeros((values.shape[1], values.shape[1]), jnp.float32)
    lo = jnp.zeros_like(hi)
    for level in reversed(range(SLICES + 1)):
        picks = [i for i in range(SLICES) if 0 <= level - i < SLICES]
        for group in [picks] if joined else [[i] for i in picks]:
            term = jnp.dot(
                jnp.concatenate([left[i] for i in group], axis=1),
                jnp.concatenate([right[level - i] for i in group], axis=0),
                preferred_element_type=jnp.float32,
            )
            total = hi + term
            back = total - hi
            lo = lo + ((hi - (total - back)) + (term - back))
            hi = total
    return hi, lo


def pack(square):
    n = square.shape[0]
    row = lax.broadcasted_iota(jnp.int32, (n // 2, n), 0)
    col = lax.broadcasted_iota(jnp.int32, (n // 2, n), 1)
    last = pltpu.roll(square[n // 2 :], n // 2, 1)
    diagonal = jnp.sum(jnp.where(col == row, last, 0.0), axis=0, keepdims=True)
    tail = jnp.where(lax.broadcasted_iota(jnp.int32, (16, n), 0) == 0, diagonal, 0.0)
    return jnp.concatenate([jnp.where(col >= row, square[: n // 2], last), tail], axis=0)


def unpack(packed):
    n = packed.shape[1]
    row = lax.broadcasted_iota(jnp.int32, (n, n), 0)
    col = lax.broadcasted_iota(jnp.int32, (n, n), 1)
    diagonal = pltpu.roll(packed[n // 2 : n // 2 + 8], n // 2, 1)[0:1]
    whole = jnp.concatenate([packed[: n // 2], jnp.zeros((n // 2, n), jnp.float32)], axis=0)
    flipped = whole.T
    low = pltpu.roll(pltpu.roll(whole, n // 2, 0), n // 2, 1)
    low_flipped = pltpu.roll(pltpu.roll(flipped, n // 2, 0), n // 2, 1)
    last = jnp.where(col < row, low, jnp.where(col == row, diagonal, low_flipped))
    below = jnp.where(col < n // 2, flipped, last)
    return jnp.where(row < n // 2, jnp.where(col >= row, whole, flipped), below)


def gram_kernel(table_ref, range_ref, kept_ref, given_ref):
    rows = kept_ref.shape[1]
    first = table_ref[12] == 0
    for i, square in enumerate(exact_gram(range_ref[...].T, False)):
        packed = pack(square)
        kept_ref[i] = jnp.where(first, packed[:rows], packed[rows:])
        given_ref[i] = jnp.where(first, packed[rows:], packed[:rows])


def exact_dot(a, b):
    return lax.dot_general(
        a,
        b,
        (((1,), (0,)), ((), ())),
        precision=lax.Precision.HIGHEST,
        preferred_element_type=jnp.float32,
    )


def short_dot(a, b):
    a, b = a.astype(jnp.bfloat16), b.astype(jnp.bfloat16)
    return jnp.dot(a, b, preferred_element_type=jnp.float32)


def eliminate(matrix, a_ref, b_ref):
    n = matrix.shape[0]
    row = lax.broadcasted_iota(jnp.int32, (n, n), 0)
    col = lax.broadcasted_iota(jnp.int32, (n, n), 1)
    a_ref[...] = matrix
    b_ref[...] = (row == col).astype(jnp.float32)
    column_row = lax.broadcasted_iota(jnp.int32, (n, 1), 0)
    panel_row = lax.broadcasted_iota(jnp.int32, (8, 1), 0)

    def block(index, carry):
        start = pl.multiple_of(index * 8, 8)
        a, b = a_ref[...], b_ref[...]
        pa, pb = a_ref[pl.ds(start, 8), :], b_ref[pl.ds(start, 8), :]
        after = column_row >= start + 8
        for t in range(8):
            lane = jnp.broadcast_to(pa[:, t : t + 1], (8, n))
            inverse = 1.0 / lane[t : t + 1]
            ra, rb = pa[t : t + 1], pb[t : t + 1]
            if t < 7:
                masked = jnp.where(panel_row > t, lane, 0.0)
                pa, pb = pa - (masked * ra) * inverse, pb - (masked * rb) * inverse
            factor = jnp.where(after, a[:, t : t + 1], 0.0)
            a, b = a - (factor * ra) * inverse, b - factor * (rb * inverse)
        a_ref[...] = pltpu.roll(a, n - 8, 1)
        b_ref[...] = b
        a_ref[pl.ds(start, 8), :] = pltpu.roll(pa, n - 8, 1)
        b_ref[pl.ds(start, 8), :] = pb
        return carry

    lax.fori_loop(0, n // 8, block, 0)
    upper = jnp.where(col >= row, a_ref[...], 0.0)
    pivot = jnp.sum(jnp.where(col == row, upper, 0.0), axis=1, keepdims=True)
    root = lax.rsqrt(pivot)
    return upper * root, b_ref[...] * root


def factor_kernel(scale, count, table_ref, half_ref, other_ref, basis_ref, norms_ref, a_ref, b_ref, out_ref):
    first = table_ref[12] == 0
    squares = []
    for i in range(2):
        above = jnp.where(first, half_ref[i], other_ref[i])
        below = jnp.where(first, other_ref[i], half_ref[i])
        squares.append(unpack(jnp.concatenate([above, below], axis=0)))
    hi, lo = squares
    n = hi.shape[0]
    row = lax.broadcasted_iota(jnp.int32, (n, n), 0)
    col = lax.broadcasted_iota(jnp.int32, (n, n), 1)
    eye = row == col
    total = hi + lo
    lo = (hi - total) + lo
    hi = total
    diagonal = jnp.sum(jnp.where(eye, hi, 0.0), axis=0, keepdims=True)
    norms_ref[...] = 0.1 * jnp.log(diagonal / count)
    upper, below = eliminate(hi, a_ref, b_ref)
    back_hi, back_lo = exact_gram(upper, True)
    rest = ((hi - back_hi) - back_lo) + lo
    above = below.T
    rest = exact_dot(exact_dot(below, rest), above)
    size = jnp.sum(rest * rest)

    @pl.when(size < 0.002)
    def _():
        half = jnp.where(eye, 0.5, jnp.where(col > row, 1.0, 0.0))
        step = half * rest
        for _ in range(3):
            step = half * (rest - short_dot(step.T, step))
        square = short_dot(step, step)
        inverse = eye.astype(jnp.float32) - step
        inverse = inverse + short_dot(inverse, square)
        out_ref[...] = inverse + short_dot(inverse, short_dot(square, square))

    @pl.when(jnp.logical_not(size < 0.002))
    def _():
        _, small = eliminate(eye.astype(jnp.float32) + rest, a_ref, b_ref)
        out_ref[...] = small.T

    basis_ref[...] = scale * exact_dot(above, out_ref[...])


def local_gram(table, range_columns):
    width = range_columns.shape[0]
    return pl.pallas_call(
        gram_kernel,
        in_specs=[SCALARS, ONCHIP],
        out_specs=[ONCHIP] * 2,
        out_shape=[jax.ShapeDtypeStruct((2, width // 4 + 8, width), jnp.float32)] * 2,
        compiler_params=LIMIT,
        name="local_gram",
    )(table, range_columns)


def two_factors(table, half, other, total_snps):
    width = half.shape[2]
    return pl.pallas_call(
        functools.partial(factor_kernel, math.sqrt(total_snps), float(total_snps)),
        in_specs=[SCALARS] + [ONCHIP] * 2,
        out_shape=(
            jax.ShapeDtypeStruct((width, width), jnp.float32),
            jax.ShapeDtypeStruct((1, width), jnp.float32),
        ),
        scratch_shapes=[pltpu.VMEM((width, width), jnp.float32)] * 3,
        compiler_params=LIMIT,
        name="two_factors",
    )(table, half, other)


STEPS = 2
CHUNKS = 16


def resident(shape, dtype=jnp.float32):
    return pltpu.VMEM(shape, dtype)


def onchip(value):
    return pltpu.with_memory_space_constraint(value, pltpu.VMEM)


def offchip(value):
    return pltpu.with_memory_space_constraint(value, pltpu.HBM)


def stats_kernel(table_ref, source_ref, held_ref, out_ref, sems):
    samples, width = source_ref.shape
    rows = samples // CHUNKS

    def copy(i):
        part = pl.ds(pl.multiple_of(i * rows, rows), rows)
        return pltpu.make_async_copy(source_ref.at[part], held_ref.at[part], sems.at[i])

    for i in range(CHUNKS):
        copy(i).start()

    def add(i, sums):
        copy(i).wait()
        values = held_ref[pl.ds(pl.multiple_of(i * rows, rows), rows), :].astype(jnp.float32)
        values = values.reshape(rows // 8, 8, width)
        return sums[0] + jnp.sum(values, axis=0), sums[1] + jnp.sum(values * values, axis=0)

    zero = jnp.zeros((8, width), jnp.float32)
    first, square = lax.fori_loop(0, CHUNKS, add, (zero, zero))
    first = jnp.sum(first, axis=0, keepdims=True)
    square = jnp.sum(square, axis=0, keepdims=True)
    whole = first.astype(jnp.int32)
    exact = samples * square.astype(jnp.int32) - whole * whole
    spread = exact.astype(jnp.float32) / float(samples * samples)
    out_ref[0:1] = first / float(samples)
    out_ref[1:2] = lax.rsqrt(jnp.sqrt(jnp.sqrt(spread + 1e-05)))


def dosage_stats(table, genotypes):
    samples, width = genotypes.shape
    return pl.pallas_call(
        stats_kernel,
        in_specs=[SCALARS, pl.BlockSpec(memory_space=pltpu.HBM)],
        out_specs=[ONCHIP] * 2,
        out_shape=[resident((samples, width), genotypes.dtype), resident((2, width))],
        scratch_shapes=[pltpu.SemaphoreType.DMA((CHUNKS,))],
        compiler_params=LIMIT,
        name="dosage_stats",
    )(table, offchip(genotypes))


def scaled_rows(held_ref, stats_ref, start, rows):
    dosages = held_ref[pl.ds(pl.multiple_of(start, rows), rows), :].astype(jnp.float32)
    return ((dosages - stats_ref[0:1]) * stats_ref[1:2]).astype(jnp.bfloat16)


def sum_kernel(table_ref, zero_ref, one_ref, two_ref, three_ref, *out_refs):
    rows = out_refs[0].shape[0]
    for k, out_ref in enumerate(out_refs):
        part = pl.ds(pl.multiple_of(table_ref[8 + k] * rows, rows), rows)
        out_ref[...] = (zero_ref[part] + two_ref[part]) + (one_ref[part] + three_ref[part])


def sum_quarter(table, got):
    rows, width = got[0].shape
    return pl.pallas_call(
        sum_kernel,
        in_specs=[SCALARS] + [ONCHIP] * 4,
        out_specs=[ONCHIP] * 4,
        out_shape=[resident((rows // 4, width))] * 4,
        compiler_params=LIMIT,
        name="sum_quarter",
    )(table, *(onchip(got[k]) for k in range(4)))


def join_kernel(table_ref, *refs):
    *part_refs, out_ref = refs
    rows = part_refs[0].shape[0]
    for k, part_ref in enumerate(part_refs):
        start = pl.multiple_of(table_ref[8 + (4 - k) % 4] * rows, rows)
        out_ref[pl.ds(start, rows)] = part_ref[...]


def join_quarter(table, parts):
    rows, width = parts[0].shape
    return pl.pallas_call(
        join_kernel,
        in_specs=[SCALARS] + [ONCHIP] * 4,
        out_specs=ONCHIP,
        out_shape=resident((4 * rows, width)),
        compiler_params=LIMIT,
        name="join_quarter",
    )(table, *(onchip(part) for part in parts))


def sketch_kernel(k, table_ref, held_ref, stats_ref, probes_ref, kept_ref, given_ref):
    whole = kept_ref.shape[0]
    rows = whole // STEPS

    def step(i, carry):
        part = pl.ds(pl.multiple_of(i * rows, rows), rows)
        for slot, target in ((4 + k, given_ref), (k, kept_ref)):
            scaled = scaled_rows(held_ref, stats_ref, table_ref[slot] * whole + i * rows, rows)
            target[part, :] = jnp.dot(scaled, probes_ref[...], preferred_element_type=jnp.float32)
        return carry

    lax.fori_loop(0, STEPS, step, 0)


def sketch_piece(k, table, held, stats, probes):
    samples, snps = held.shape
    width = probes.shape[1]
    return pl.pallas_call(
        functools.partial(sketch_kernel, k),
        in_specs=[SCALARS, ONCHIP, ONCHIP, ONCHIP],
        out_specs=[ONCHIP] * 2,
        out_shape=[resident((samples // 8, width))] * 2,
        compiler_params=LIMIT,
        cost_estimate=pl.CostEstimate(
            flops=samples // 2 * snps * width, transcendentals=0, bytes_accessed=samples * snps // 2
        ),
        name="sketch_piece",
    )(table, held, stats, probes)


def range_kernel(k, table_ref, held_ref, stats_ref, mine_ref, theirs_ref, acc_ref, out_ref):
    width = acc_ref.shape[0]
    whole = mine_ref.shape[0]
    rows = whole // STEPS
    out_ref[...] = acc_ref[...]

    def step(i, carry):
        part = pl.ds(pl.multiple_of(i * rows, rows), rows)
        for slot, sketch_ref in ((k, mine_ref), (4 + k, theirs_ref)):
            sketch = sketch_ref[part, :].T
            high = sketch.astype(jnp.bfloat16)
            rest = sketch - high.astype(jnp.float32)
            mid = rest.astype(jnp.bfloat16)
            low = (rest - mid.astype(jnp.float32)).astype(jnp.bfloat16)
            parts = jnp.concatenate([high, mid, low], axis=0)
            scaled = scaled_rows(held_ref, stats_ref, table_ref[slot] * whole + i * rows, rows)
            product = jnp.dot(parts, scaled, preferred_element_type=jnp.float32)
            out_ref[...] += product[:width] + product[width : 2 * width] + product[2 * width :]
        return carry

    lax.fori_loop(0, STEPS, step, 0)


def range_piece(k, table, held, stats, mine, theirs, acc):
    samples, snps = held.shape
    width = mine.shape[1]
    return pl.pallas_call(
        functools.partial(range_kernel, (4 - k) % 4),
        in_specs=[SCALARS] + [ONCHIP] * 5,
        out_specs=ONCHIP,
        out_shape=resident((width, snps)),
        compiler_params=LIMIT,
        cost_estimate=pl.CostEstimate(
            flops=3 * samples // 2 * snps * width, transcendentals=0, bytes_accessed=samples * snps // 2
        ),
        name="range_piece",
    )(table, held, stats, onchip(mine), onchip(theirs), acc)


def solution(mesh):
    nx = mesh.shape["chrom"]
    nz = mesh.shape["snp"] // 8
    torus = Torus((nx, nz, 4, 2))
    fine = Mesh(mesh.devices.reshape(torus.sizes), AXES)

    def body(genotypes, probes):
        samples, snps = genotypes.shape
        width = probes.shape[1]
        total_snps = snps * fine.size
        core, one, two = torus.places()
        turns = jnp.arange(4, dtype=jnp.int32)
        table = jnp.concatenate(
            [
                core * 4 + ((one + turns) & 3),
                (1 - core) * 4 + ((two + turns) & 3),
                (two + turns) & 3,
                core[None],
            ]
        ).astype(jnp.int32)
        held, stats = (onchip(v) for v in dosage_stats(table, genotypes))
        got = {}
        for k in (2, 1, 3, 0):
            kept, given = sketch_piece(k, table, held, stats, probes)
            piece = kept + torus.core(given)
            got[k] = torus.first(piece, k) if k else piece
        split = sum_quarter(table, got)
        got = [torus.second(split[k], k) for k in (1, 2, 3)]
        small = (split[0] + got[1]) + (got[0] + got[2])
        small = small.reshape(nz, samples // 32 // nz, width)
        own = lax.all_to_all(small, "z", 0, 0)
        own = tree_sum([own[i] for i in range(nz)], jnp.add)
        small = lax.all_to_all(jnp.broadcast_to(own, (nz, *own.shape)), "z", 0, 0)
        small = small.reshape(samples // 32, width)
        quarter = join_quarter(table, [small] + [torus.second(small, k) for k in (1, 2, 3)])
        mine = {0: quarter}
        for k in (1, 3, 2):
            mine[k] = torus.first(quarter, k)
        acc = jnp.zeros((width, snps), jnp.float32)
        for k in (0, 1, 3, 2):
            theirs = torus.core(mine[k])
            acc = range_piece(k, table, held, stats, mine[k], theirs, acc)
        half, other = sum_square(torus, *local_gram(table, acc))
        basis, range_log_norms = two_factors(table, half, other, total_snps)
        unit_basis = lax.dot_general(
            acc,
            basis,
            (((0,), (0,)), ((), ())),
            precision=lax.Precision.HIGHEST,
            preferred_element_type=jnp.float32,
        )
        return (unit_basis, range_log_norms[0])

    return jax.shard_map(
        body,
        mesh=fine,
        in_specs=(P(None, AXES), P(AXES, None)),
        out_specs=(P(AXES, None), P()),
        check_vma=False,
    )
```
